32 devices in a mesh: groups: 2 (over y), rows: 4 (over z), feat: 4 (over x, core).
Axes of the slice: x: 2, y: 2, z: 4, core: 2. Of those that a mesh axis runs over, the one named last changes fastest.
Arguments:
- student: float32 [1280, 4096], P(('groups', 'rows'), 'feat'), parts along dimension 0, may hold values from -1 to 1
- teacher: bfloat16 [1280, 1024], P(('groups', 'rows'), 'feat'), parts along dimension 0, may hold values from -1 to 1
Outputs:
- row_loss: float32 [1280], P(('groups', 'rows')), parts along dimension 0
- student_grad: float32 [1280, 4096], P(('groups', 'rows'), 'feat'), parts along dimension 0
The draws below stay inside these ranges and needn't reach their ends.
There are 2 independent parts, one for each index of `groups`. The reference program is written for one: setup_inputs(seed, part) draws one part's arguments, and reference() takes and returns one part's arrays. A program takes and returns all parts, laid end to end along the dimension named above; each array names one. Nothing has to cross between parts.
All inputs are finite; a program needn't handle non-finite values.
Results may differ from the reference program's by a relative error of at most 0.0085.
Values may be sent and summed in bfloat16 or wider, within the bound.
A program may use at most 64 MiB of HBM per device.

```python
import math
import jax
import jax.numpy as jnp
from jax import lax

D = 4096
DT = 1024
EMBEDS = 640
N_FEAT = 4


def draw_student(key, part):
    keys = jax.random.split(jax.random.fold_in(key, 11), 3)
    row_scale = jnp.exp(jax.random.uniform(keys[0], (EMBEDS, 1), jnp.float32) * math.log(10.0))
    col_scale = jnp.exp(jax.random.uniform(keys[1], (1, D), jnp.float32) * math.log(10.0))
    base = jnp.clip(jax.random.normal(keys[2], (EMBEDS, D), jnp.float32), -4.0, 4.0)
    return (base * row_scale * col_scale * (0.02 / math.sqrt(D))).astype(jnp.float32)


def draw_teacher(key, part):
    keys = jax.random.split(jax.random.fold_in(key, 23), 1)
    base = jnp.clip(jax.random.normal(keys[0], (EMBEDS, DT), jnp.float32), -4.0, 4.0)
    return (base / math.sqrt(DT)).astype(jnp.bfloat16)


def setup_inputs(seed: int = 0, part: int = 0) -> dict:
    splits = jax.random.split(jax.random.key(seed), 3)
    part_splits = jax.random.split(jax.random.fold_in(splits[2], part), 3)
    student = draw_student(jax.random.fold_in(jax.random.fold_in(splits[2], part), 71), part)
    teacher = draw_teacher(jax.random.fold_in(jax.random.fold_in(splits[2], part), 71), part)
    return dict(student=student, teacher=teacher)


EPSILON = 1e-06

def reference(student, teacher):
    squares = lax.optimization_barrier(jnp.sum(student * student, axis=1))
    scaling = lax.rsqrt(squares + EPSILON)
    unit = student * scaling[:, None]
    unit_half = unit.astype(jnp.bfloat16)
    slice_width = D // N_FEAT
    teach_width = DT // N_FEAT
    block_rows = math.gcd(512, EMBEDS)
    contract = (((1,), (1,)), ((), ()))

    def one_block(start):
        mine = lax.dynamic_slice_in_dim(unit_half, start, block_rows, 0)
        mine_teacher = lax.dynamic_slice_in_dim(teacher, start, block_rows, 0)
        differ = jnp.zeros((block_rows, EMBEDS), jnp.float32)
        for feature_slice in range(N_FEAT):
            lower = feature_slice * slice_width
            upper = lower + slice_width
            tlower = feature_slice * teach_width
            tupper = tlower + teach_width
            student_term = lax.dot_general(mine[:, lower:upper], unit_half[:, lower:upper], contract, preferred_element_type=jnp.float32)
            teacher_term = lax.dot_general(mine_teacher[:, tlower:tupper], teacher[:, tlower:tupper], contract, preferred_element_type=jnp.float32)
            term = lax.optimization_barrier((student_term - teacher_term).astype(jnp.bfloat16)).astype(jnp.float32)
            differ = differ + term
        losses = lax.optimization_barrier(jnp.sum(differ * differ, axis=1))
        pulled = jnp.dot(differ.astype(jnp.bfloat16), unit_half, preferred_element_type=jnp.float32)
        return (losses, pulled)
    starts = jnp.arange(EMBEDS // block_rows, dtype=jnp.int32) * block_rows
    losses, pulled = lax.map(one_block, starts)
    losses = losses.reshape(EMBEDS)
    pulled = pulled.reshape(EMBEDS, D)
    radial = lax.optimization_barrier(jnp.sum(pulled * unit, axis=1))
    factor = 4.0 * D / EMBEDS
    student_grad = factor * scaling[:, None] * (pulled - radial[:, None] * unit)
    return (D / EMBEDS * losses, student_grad)
```

```python
import functools

import jax
import jax.numpy as jnp
from jax import lax
from jax.experimental import pallas as pl
from jax.experimental.pallas import tpu as pltpu
from jax.sharding import PartitionSpec as P

D = 4096
EPSILON = 1e-06
CHUNK = 32
LAST = (((1,), (1,)), ((), ()))
FIRST = (((0,), (0,)), ((), ()))
F32 = jnp.float32
BF16 = jnp.bfloat16
MESH = pl.DeviceIdType.MESH


def shifted(block, axis, distance):
    devices = range(lax.axis_size(axis))
    route = [((i - distance) % len(devices), i) for i in devices]
    return lax.ppermute(block, axis, route)


def ring(student, teacher):
    cycle = lax.axis_size("rows")
    rows_here = student.shape[0]
    width = student.shape[1]
    embeds = rows_here * cycle
    squares = lax.psum(jnp.sum(student * student, axis=1), "feat")
    scaling = lax.rsqrt(squares + EPSILON)
    unit = student * scaling[:, None]
    unit_half = unit.astype(BF16)
    packed = jnp.concatenate([unit_half, teacher], axis=1)

    def absorb(carry, visitor):
        losses, pulled = carry
        other_unit = visitor[:, :width]
        other_teacher = visitor[:, width:]
        student_term = lax.dot_general(
            unit_half, other_unit, LAST, preferred_element_type=F32
        )
        teacher_term = lax.dot_general(
            teacher, other_teacher, LAST, preferred_element_type=F32
        )
        differ = lax.psum((student_term - teacher_term).astype(BF16), "feat").astype(F32)
        losses = losses + jnp.sum(differ * differ, axis=1)
        pulled = pulled + jnp.dot(
            differ.astype(BF16), other_unit, preferred_element_type=F32
        )
        return (losses, pulled)

    carry = (jnp.zeros((rows_here,), F32), jnp.zeros((rows_here, width), F32))
    carry = absorb(carry, packed)

    def turn(step, state):
        inner, visitor = state
        visitor = shifted(visitor, "rows", 1)
        return (absorb(inner, visitor), visitor)

    carry, visitor = lax.fori_loop(0, cycle - 1, turn, (carry, packed))
    losses, pulled = carry
    radial = lax.psum(jnp.sum(pulled * unit, axis=1), "feat")
    factor = 4.0 * D / embeds
    student_grad = factor * scaling[:, None] * (pulled - radial[:, None] * unit)
    return (D / embeds * losses, student_grad)


def kernel(
    R, F, NC, x_hbm, t_hbm, loss_ref, g_ref,
    x_ref, X, T, SQ, S, CX, TP, TQ, TS, TR, TE, TG, rad_ref,
    ins, xs, xr, ts, tr, ss, sr, qs, qr, cs, cr, g1s, g1r, g2s, g2r, g3s, g3r, g4s, g4r, g5s, g5r,
):
    z = lax.axis_index("rows")
    f = lax.axis_index("feat")
    core = lax.rem(f, 2)
    chip = lax.div(f, 2)
    n, w = x_ref.shape
    rc = n // NC
    side = lax.div(z, 2)
    mate = z + 1 - 2 * lax.rem(z, 2)
    is_hub = jnp.logical_or(z == 1, z == 2)
    is_end = jnp.logical_not(is_hub)
    IN, OUT = 0, 1

    bar = pltpu.get_barrier_semaphore()
    for p in range(1, F):
        pl.semaphore_signal(
            bar, inc=1, device_id={"feat": lax.rem(f + p, F)}, device_id_type=MESH
        )
    pl.semaphore_signal(bar, inc=1, device_id={"rows": mate}, device_id_type=MESH)

    @pl.when(is_hub)
    def _():
        pl.semaphore_signal(bar, inc=1, device_id={"rows": R - 1 - z}, device_id_type=MESH)

    x_in = pltpu.make_async_copy(x_hbm, x_ref, ins.at[0])
    t_in = pltpu.make_async_copy(t_hbm, T.at[z], ins.at[1])
    x_in.start()
    t_in.start()

    eye = lax.broadcasted_iota(jnp.int32, (n, n), 0) == lax.broadcasted_iota(
        jnp.int32, (n, n), 1
    )

    def to_row(column):
        return jnp.sum(jnp.where(eye, column, 0.0), axis=0, keepdims=True)

    def to_column(row):
        return jnp.sum(jnp.where(eye, row, 0.0), axis=1, keepdims=True)

    x_in.wait()
    x = x_ref[...]
    X[z] = x.astype(BF16).reshape(NC, rc, w)
    SQ[f] = jnp.broadcast_to(to_row(jnp.sum(x * x, axis=1, keepdims=True)), (8, n))
    t_in.wait()
    pl.semaphore_wait(bar, F + is_hub.astype(jnp.int32))

    def remote(src, dst, send, recv, device):
        return pltpu.make_async_remote_copy(
            src_ref=src, dst_ref=dst, send_sem=send, recv_sem=recv,
            device_id=device, device_id_type=MESH,
        )

    def across(entry, index, send, recv, p, mine):
        ref = entry(f if mine else lax.rem(f + F - p, F))
        return remote(
            ref, ref, send.at[index + (p - 1,)], recv.at[index + (p - 1,)],
            {"feat": lax.rem(f + p, F)},
        )

    def spread(entry, index, send, recv):
        for p in range(1, F):
            across(entry, index, send, recv, p, True).start()

    def collect(entry, index, send, recv):
        for p in range(1, F):
            across(entry, index, send, recv, p, False).wait_recv()

    def drained(entry, index, send, recv):
        for p in range(1, F):
            across(entry, index, send, recv, p, True).wait_send()

    squares_of = lambda g: SQ.at[g]
    feat_x = {"feat": lax.rem(f + 2, F)}
    feat_sib = {"feat": f + 1 - 2 * core}
    feat_diag = {"feat": F - 1 - f}

    def program(hub):
        started = []

        def device(d):
            if not hub or d == OUT:
                return {"rows": mate}
            return {"rows": R - 1 - z}

        def x_copy(d, src, c):
            ref = X.at[src, c]
            return remote(ref, ref, xs.at[d, src, c], xr.at[src, c], device(d))

        def t_copy(src):
            ref = T.at[src]
            return remote(ref, ref, ts.at[src], tr.at[src], device(IN))

        def s_copy(d, src):
            ref = S.at[src]
            return remote(ref, ref, ss.at[d, src], sr.at[src], device(d))

        def go(copy):
            copy.start()
            started.append(copy)

        groups = []

        def entry_of(src, c, k):
            return lambda g: CX.at[g, src, pl.ds(c, k)]

        def gram(src, c=0, k=NC):
            CX[f, src, pl.ds(c, k)] = (
                lax.dot_general(
                    X[src, pl.ds(c, k)].reshape(k * rc, w), X[z].reshape(n, w),
                    LAST, preferred_element_type=F32,
                ).astype(BF16).reshape(k, rc, n)
            )
            slot = len(groups)
            groups.append((entry_of(src, c, k), (slot,)))
            spread(*groups[slot], cs, cr)
            return slot, src, c, k

        def finish(piece, first=False):
            slot, src, c, k = piece
            collect(*groups[slot], cs, cr)
            m = k * rc
            raw = CX[0, src, pl.ds(c, k)].astype(F32)
            for g in range(1, F):
                raw = raw + CX[g, src, pl.ds(c, k)].astype(F32)
            half_way = raw.reshape(m, n) * S[z][:1]
            here = lax.broadcasted_iota(jnp.int32, (m, n), 0) + c * rc == (
                lax.broadcasted_iota(jnp.int32, (m, n), 1)
            )
            column = jnp.sum(jnp.where(here, S[src][:1], 0.0), axis=1, keepdims=True)
            differ = half_way * column - TG[src, pl.ds(c * rc, m)].astype(F32)
            half = (differ * column).astype(BF16)
            loss = jnp.sum(differ * differ, axis=0, keepdims=True)
            radial = jnp.sum(half.astype(F32) * half_way, axis=0, keepdims=True)
            pulled = lax.dot_general(
                half, X[src, pl.ds(c, k)].reshape(m, w), FIRST, preferred_element_type=F32
            )
            if first:
                loss_ref[...] = loss
                rad_ref[...] = radial
                g_ref[...] = pulled
            else:
                loss_ref[...] += loss
                rad_ref[...] += radial
                g_ref[...] += pulled

        def scale():
            collect(squares_of, (), qs, qr)
            squares = SQ[0]
            for g in range(1, F):
                squares = squares + SQ[g]
            S[z] = lax.rsqrt(squares + EPSILON)
            go(s_copy(IN, z))
            if hub:
                go(s_copy(OUT, z))

        def pair(which):
            return pl.ds(2 * (side if which == 0 else 1 - side), 2)

        def teach_1(ph):
            both = T[pair(ph)].reshape(2 * n, -1)
            for k, row in ((0, z), (1, mate)):
                TP[ph, k] = lax.dot_general(
                    both, T[row], LAST, preferred_element_type=F32
                ).astype(BF16).reshape(2, n, n)
            go(remote(TP.at[ph, 1 - core], TQ.at[ph], g1s.at[ph], g1r.at[ph], feat_sib))

        def teach_2(ph):
            remote(TP.at[ph, core], TQ.at[ph], g1s.at[ph], g1r.at[ph], feat_sib).wait_recv()
            TS[ph] = (TP[ph, core].astype(F32) + TQ[ph].astype(F32)).astype(BF16)

            @pl.when(core == 0)
            def _():
                remote(TS.at[ph], TR.at[ph], g2s.at[ph], g2r.at[ph], feat_x).start()

            @pl.when(core == 1)
            def _():
                part = (ph, 1 - chip)
                remote(TS.at[part], TR.at[part], g2s.at[ph], g2r.at[ph], feat_x).start()

        def own_half(ph):
            ref = TG.at[pair(ph)]
            return remote(ref, ref, g3s.at[ph], g3r.at[ph], feat_sib)

        def end_part(ph):
            into = TG.at[2 * (side if ph == 0 else 1 - side) + chip]
            return remote(TE.at[ph], into, g4s.at[ph], g4r.at[ph], {"rows": mate})

        def teach_3(ph):
            @pl.when(core == 0)
            def _():
                remote(TS.at[ph], TR.at[ph], g2s.at[ph], g2r.at[ph], feat_x).wait()
                TG[pair(ph)] = (TS[ph].astype(F32) + TR[ph].astype(F32)).astype(BF16)
                own_half(ph).start()

            @pl.when(core == 1)
            def _():
                part = (ph, 1 - chip)
                remote(TS.at[part], TR.at[part], g2s.at[ph], g2r.at[ph], feat_x).wait_send()
                part = (ph, chip)
                remote(TS.at[part], TR.at[part], g2s.at[ph], g2r.at[ph], feat_x).wait_recv()
                TE[ph] = (TS[ph, chip].astype(F32) + TR[ph, chip].astype(F32)).astype(BF16)
                end_part(ph).start()

        def teach_4(ph):
            @pl.when(core == 1)
            def _():
                own_half(ph).wait_recv()

        def learn_part(ph, k, which):
            ref = TG.at[2 * (side if ph == 0 else 1 - side) + which]
            to = (feat_sib, feat_x, feat_diag)[k]
            return remote(ref, ref, g5s.at[ph, k], g5r.at[ph, min(k, 1)], to)

        def learn_1(ph):
            @pl.when(core == 1)
            def _():
                end_part(ph).wait_recv()
                for k in range(3):
                    learn_part(ph, k, chip).start()

        def learn_2(ph):
            @pl.when(core == 0)
            def _():
                learn_part(ph, 0, chip).wait_recv()
            learn_part(ph, 1, 1 - chip).wait_recv()

        spread(squares_of, (), qs, qr)
        if hub:
            far, last = R - 1 - z, R - 1 - mate
            go(t_copy(z))
            for c in range(NC):
                go(x_copy(OUT, z, c))
            go(x_copy(IN, z, 0))
            own = gram(z)
            t_copy(mate).wait_recv()
            go(t_copy(mate))
            for c in range(1, NC):
                go(x_copy(IN, z, c))
            teach_1(0)
            scale()
            near_in = lambda c: (x_copy(OUT, mate, c).wait_recv(), go(x_copy(IN, mate, c)))
            far_out = lambda src, c: (x_copy(IN, src, c).wait_recv(), go(x_copy(OUT, src, c)))
            near_in(0)
            teach_2(0)
            far_out(far, 0)
            near_in(1)
            t_copy(far).wait_recv()
            t_copy(last).wait_recv()
            teach_1(1)
            near_in(2)
            far_out(far, 1)
            s_copy(IN, mate).wait_recv()
            go(s_copy(IN, mate))
            s_copy(IN, far).wait_recv()
            go(s_copy(OUT, far))
            teach_3(0)
            teach_2(1)
            near_in(3)
            far_out(far, 2)
            near_in(4)
            second = gram(mate)
            far_out(far, 3)
            s_copy(IN, last).wait_recv()
            go(s_copy(OUT, last))
            teach_4(0)
            finish(own, first=True)
            teach_3(1)
            far_out(far, 4)
            third = gram(far)
            far_out(last, 0)
            finish(second)
            far_out(last, 1)
            teach_4(1)
            finish(third)
            far_out(last, 2)
            pieces = [gram(last, 0, 3)]
            far_out(last, 3)
            pieces.append(gram(last, 3, 1))
            finish(pieces[0])
            far_out(last, 4)
            pieces.append(gram(last, 4, 1))
            finish(pieces[1])
            finish(pieces[2])
        else:
            far, last = R - 1 - mate, R - 1 - z

            def here(src, *chunks):
                for c in chunks:
                    x_copy(IN, src, c).wait_recv()

            go(t_copy(z))
            for c in range(NC):
                go(x_copy(IN, z, c))
            own = gram(z)
            scale()
            here(mate, *range(NC))
            second = gram(mate)
            s_copy(IN, mate).wait_recv()
            learn_1(0)
            here(far, 0, 1)
            learn_2(0)
            finish(own, first=True)
            finish(second)
            here(far, 2, 3, 4)
            third = gram(far)
            s_copy(IN, far).wait_recv()
            s_copy(IN, last).wait_recv()
            learn_1(1)
            here(last, 0, 1)
            learn_2(1)
            finish(third)
            here(last, 2)
            pieces = [gram(last, 0, 3)]
            here(last, 3)
            pieces.append(gram(last, 3, 1))
            finish(pieces[0])
            here(last, 4)
            pieces.append(gram(last, 4, 1))
            finish(pieces[1])
            finish(pieces[2])

        drained(squares_of, (), qs, qr)
        for group in groups:
            drained(*group, cs, cr)
        for copy in started:
            copy.wait_send()
        for ph in range(2):
            if hub:
                @pl.when(core == 0)
                def _():
                    own_half(ph).wait_send()

                @pl.when(core == 1)
                def _():
                    end_part(ph).wait_send()
            else:
                @pl.when(core == 1)
                def _():
                    for k in range(3):
                        learn_part(ph, k, chip).wait_send()

    @pl.when(is_hub)
    def _():
        program(True)

    @pl.when(is_end)
    def _():
        program(False)

    factor = 4.0 * D / (n * R)
    loss_ref[...] = (D / (n * R)) * loss_ref[...]
    scaling = to_column(S[z][:1])
    radial = to_column(rad_ref[...])
    g_ref[...] = (factor * scaling) * (g_ref[...] - (radial * scaling) * x_ref[...])


def fused(R, F, student, teacher):
    n, w = student.shape
    wt = teacher.shape[1]
    NC = n // CHUNK
    dma = pltpu.SemaphoreType.DMA
    vmem = pl.BlockSpec(memory_space=pltpu.VMEM)
    hbm = pl.BlockSpec(memory_space=pltpu.HBM)
    loss, grad = pl.pallas_call(
        functools.partial(kernel, R, F, NC),
        out_shape=(
            jax.ShapeDtypeStruct((1, n), F32),
            jax.ShapeDtypeStruct((n, w), F32),
        ),
        in_specs=[hbm, hbm],
        out_specs=(vmem, vmem),
        scratch_shapes=[
            pltpu.VMEM((n, w), F32),
            pltpu.VMEM((R, NC, CHUNK, w), BF16),
            pltpu.VMEM((R, n, wt), BF16),
            pltpu.VMEM((F, 8, n), F32),
            pltpu.VMEM((R, 8, n), F32),
            pltpu.VMEM((F, R, NC, CHUNK, n), BF16),
            pltpu.VMEM((2, 2, 2, n, n), BF16),
            pltpu.VMEM((2, 2, n, n), BF16),
            pltpu.VMEM((2, 2, n, n), BF16),
            pltpu.VMEM((2, 2, n, n), BF16),
            pltpu.VMEM((2, n, n), BF16),
            pltpu.VMEM((R, n, n), BF16),
            pltpu.VMEM((1, n), F32),
            dma((2,)),
            dma((2, R, NC)), dma((R, NC)),
            dma((R,)), dma((R,)),
            dma((2, R)), dma((R,)),
            dma((F - 1,)), dma((F - 1,)),
            dma((8, F - 1)), dma((8, F - 1)),
            dma((2,)), dma((2,)), dma((2,)), dma((2,)), dma((2,)), dma((2,)),
            dma((2,)), dma((2,)), dma((2, 3)), dma((2, 2)),
        ],
        compiler_params=pltpu.CompilerParams(
            collective_id=0, has_side_effects=True, vmem_limit_bytes=48 * 2**20
        ),
    )(pltpu.with_memory_space_constraint(student, pltpu.HBM), pltpu.with_memory_space_constraint(teacher, pltpu.HBM))
    return loss.reshape(n), grad


def solution(mesh):
    R, F = mesh.shape["rows"], mesh.shape["feat"]
    body = functools.partial(fused, R, F) if R == 4 and F == 4 else ring
    in_specs = (P(("groups", "rows"), "feat"), P(("groups", "rows"), "feat"))
    out_specs = (P(("groups", "rows")), P(("groups", "rows"), "feat"))
    return jax.shard_map(
        body, mesh=mesh, in_specs=in_specs, out_specs=out_specs, check_vma=False
    )
```

```python
import functools

import jax
import jax.numpy as jnp
from jax import lax
from jax.experimental import pallas as pl
from jax.experimental.pallas import tpu as pltpu
from jax.sharding import PartitionSpec as P

D = 4096
EPSILON = 1e-06
CHUNK = 32
LAST = (((1,), (1,)), ((), ()))
FIRST = (((0,), (0,)), ((), ()))
F32 = jnp.float32
BF16 = jnp.bfloat16
MESH = pl.DeviceIdType.MESH


def shifted(block, axis, distance):
    devices = range(lax.axis_size(axis))
    route = [((i - distance) % len(devices), i) for i in devices]
    return lax.ppermute(block, axis, route)


def ring(student, teacher):
    cycle = lax.axis_size("rows")
    rows_here = student.shape[0]
    width = student.shape[1]
    embeds = rows_here * cycle
    squares = lax.psum(jnp.sum(student * student, axis=1), "feat")
    scaling = lax.rsqrt(squares + EPSILON)
    unit = student * scaling[:, None]
    unit_half = unit.astype(BF16)
    packed = jnp.concatenate([unit_half, teacher], axis=1)

    def absorb(carry, visitor):
        losses, pulled = carry
        other_unit = visitor[:, :width]
        other_teacher = visitor[:, width:]
        student_term = lax.dot_general(
            unit_half, other_unit, LAST, preferred_element_type=F32
        )
        teacher_term = lax.dot_general(
            teacher, other_teacher, LAST, preferred_element_type=F32
        )
        differ = lax.psum((student_term - teacher_term).astype(BF16), "feat").astype(F32)
        losses = losses + jnp.sum(differ * differ, axis=1)
        pulled = pulled + jnp.dot(
            differ.astype(BF16), other_unit, preferred_element_type=F32
        )
        return (losses, pulled)

    carry = (jnp.zeros((rows_here,), F32), jnp.zeros((rows_here, width), F32))
    carry = absorb(carry, packed)

    def turn(step, state):
        inner, visitor = state
        visitor = shifted(visitor, "rows", 1)
        return (absorb(inner, visitor), visitor)

    carry, visitor = lax.fori_loop(0, cycle - 1, turn, (carry, packed))
    losses, pulled = carry
    radial = lax.psum(jnp.sum(pulled * unit, axis=1), "feat")
    factor = 4.0 * D / embeds
    student_grad = factor * scaling[:, None] * (pulled - radial[:, None] * unit)
    return (D / embeds * losses, student_grad)


def kernel(
    R, F, NC, x_hbm, t_hbm, loss_ref, g_ref,
    x_ref, X, T, SQ, S, CX, CY, KP, TP, TQ, TE, TG, RX, DE, RL, rad_ref,
    ins, xs, xr, ts, tr, ss, sr, qs, qr, cs, cr, ps, pr, es, er, rs, rr, ds, dr,
):
    z = lax.axis_index("rows")
    f = lax.axis_index("feat")
    core = lax.rem(f, 2)
    n, w = x_ref.shape
    rc = n // NC
    HC = TE.shape[0]
    mate = z + 1 - 2 * lax.rem(z, 2)
    is_hub = jnp.logical_or(z == 1, z == 2)
    is_end = jnp.logical_not(is_hub)
    IN, OUT = 0, 1

    TG[...] = jnp.zeros_like(TG)
    bar = pltpu.get_barrier_semaphore()
    for p in range(1, F):
        pl.semaphore_signal(
            bar, inc=1, device_id={"feat": lax.rem(f + p, F)}, device_id_type=MESH
        )
    pl.semaphore_signal(bar, inc=1, device_id={"rows": mate}, device_id_type=MESH)

    @pl.when(is_hub)
    def _():
        pl.semaphore_signal(bar, inc=1, device_id={"rows": R - 1 - z}, device_id_type=MESH)

    x_in = pltpu.make_async_copy(x_hbm, x_ref, ins.at[0])
    t_in = pltpu.make_async_copy(t_hbm, T.at[z], ins.at[1])
    x_in.start()
    t_in.start()

    eye = lax.broadcasted_iota(jnp.int32, (n, n), 0) == lax.broadcasted_iota(
        jnp.int32, (n, n), 1
    )

    def to_row(column):
        return jnp.sum(jnp.where(eye, column, 0.0), axis=0, keepdims=True)

    def to_column(row):
        return jnp.sum(jnp.where(eye, row, 0.0), axis=1, keepdims=True)

    x_in.wait()
    x = x_ref[...]
    X[z] = x.astype(BF16).reshape(NC, rc, w)
    SQ[f] = jnp.broadcast_to(to_row(jnp.sum(x * x, axis=1, keepdims=True)), (8, n))
    t_in.wait()
    pl.semaphore_wait(bar, F + is_hub.astype(jnp.int32))

    def remote(src, dst, send, recv, device):
        return pltpu.make_async_remote_copy(
            src_ref=src, dst_ref=dst, send_sem=send, recv_sem=recv,
            device_id=device, device_id_type=MESH,
        )

    def spread(ref_of, send, recv):
        for p in range(1, F):
            remote(
                ref_of(f), ref_of(f), send, recv, {"feat": lax.rem(f + p, F)}
            ).start()

    def collect(ref_of, send, recv):
        ref = ref_of(pl.ds(0, F - 1))
        remote(ref, ref, send, recv, feat_x).wait_recv()

    def drained(ref, send, recv):
        remote(ref, ref, send, recv, feat_x).wait_send()

    squares_of = lambda g: SQ.at[g]
    feat_x = {"feat": lax.rem(f + 2, F)}
    feat_sib = {"feat": f + 1 - 2 * core}

    def program(hub):
        def device(d):
            if not hub or d == OUT:
                return {"rows": mate}
            return {"rows": R - 1 - z}

        def x_copy(d, src, c):
            ref = X.at[src, c]
            return remote(ref, ref, xs.at[d], xr.at[src, c], device(d))

        def t_copy(src):
            ref = T.at[src]
            return remote(ref, ref, ts.at[0], tr.at[src], device(IN))

        def s_copy(d, src):
            ref = S.at[src]
            return remote(ref, ref, ss.at[d], sr.at[src], device(d))

        def send(d, src, *chunks):
            for c in chunks:
                x_copy(d, src, c).start()

        def here(src, *chunks):
            for c in chunks:
                x_copy(IN, src, c).wait_recv()

        def relay(d, src, c):
            here(src, c)
            send(d, src, c)

        groups = []

        def spot(c, m):
            return lax.broadcasted_iota(jnp.int32, (m, n), 0) + c * rc == (
                lax.broadcasted_iota(jnp.int32, (m, n), 1)
            )

        def column_of(src, c, m):
            return jnp.sum(jnp.where(spot(c, m), S[src][:1], 0.0), axis=1, keepdims=True)

        def exchange(ref_of, send_sem):
            slot = len(groups)
            groups.append(ref_of)
            spread(ref_of, send_sem, cr.at[slot])
            return slot

        def gram(src, place, c=0, k=NC, both=None):
            m = k * rc
            cosine = S[z][:1] * lax.dot_general(
                X[src, pl.ds(c, k)].reshape(m, w), X[z].reshape(n, w),
                LAST, preferred_element_type=F32,
            )
            if hub or place == 0:
                teacher = lax.dot_general(
                    T[src, pl.ds(c * rc, m)], T[z], LAST, preferred_element_type=F32
                )
            else:
                at = [(place - 1) * NC + c + q for q in range(k)]
                teacher = jnp.concatenate([TG[q // HC, q % HC] for q in at]).astype(F32)
            term = cosine * column_of(src, c, m) - teacher
            CX[f, src, pl.ds(c, k)] = term.astype(BF16).reshape(k, rc, n)
            slots = [exchange(lambda g: CX.at[g, src, pl.ds(c, k)], cs.at[0])]
            if both is None:
                KP[src, pl.ds(c, k)] = cosine.reshape(k, rc, n)
            else:
                CY[f, both, pl.ds(c, k)] = cosine.astype(BF16).reshape(k, rc, n)
                slots.append(
                    exchange(lambda g: CY.at[g, both, pl.ds(c, k)], cs.at[1 + both])
                )
            return slots, src, c, k, both

        def finish(piece, first=False, deliver=False):
            slots, src, c, k, both = piece
            m = k * rc
            for slot in slots:
                collect(groups[slot], cs.at[0], cr.at[slot])
            differ = CX[0, src, pl.ds(c, k)].astype(F32)
            for g in range(1, F):
                differ = differ + CX[g, src, pl.ds(c, k)].astype(F32)
            differ = differ.reshape(m, n)
            if both is None:
                cosine = KP[src, pl.ds(c, k)]
            else:
                cosine = CY[0, both, pl.ds(c, k)].astype(F32)
                for g in range(1, F):
                    cosine = cosine + CY[g, both, pl.ds(c, k)].astype(F32)
            cosine = cosine.reshape(m, n)
            column = column_of(src, c, m)
            if deliver:
                DE[pl.ds(c, k)] = (differ * S[z][:1]).astype(BF16).reshape(k, rc, n)
                for q, value in enumerate((differ * cosine * column, differ * differ)):
                    value = jnp.sum(value, axis=1, keepdims=True)
                    value = jnp.sum(jnp.where(spot(c, m), value, 0.0), axis=0, keepdims=True)
                    if c == 0:
                        RL[q:q + 1] = value
                    else:
                        RL[q:q + 1] += value
                part = 0 if c == 0 else 1

                @pl.when(core == part)
                def _():
                    end_differ(part).start()

                if c > 0:
                    end_sums().start()
            half = (differ * column).astype(BF16)
            loss = jnp.sum(differ * differ, axis=0, keepdims=True)
            radial = jnp.sum(half.astype(F32) * cosine, axis=0, keepdims=True)
            pulled = lax.dot_general(
                half, X[src, pl.ds(c, k)].reshape(m, w), FIRST, preferred_element_type=F32
            )
            if first:
                loss_ref[...] = loss
                rad_ref[...] = jnp.zeros_like(radial)
                RX[f] = jnp.broadcast_to(radial, (8, n))
                g_ref[...] = pulled
            else:
                loss_ref[...] += loss
                if both is None:
                    RX[f] += radial
                else:
                    rad_ref[...] += radial
                g_ref[...] += pulled

        def part_of(part):
            return DE.at[pl.ds(0, 3)] if part == 0 else DE.at[pl.ds(3, NC - 3)]

        def end_differ(part):
            ref = part_of(part)
            return remote(ref, ref, ds.at[0], dr.at[0], {"rows": R - 1 - mate})

        def end_sums():
            return remote(RL, RL, ds.at[1], dr.at[1], {"rows": R - 1 - mate})

        def share(part):
            ref = part_of(part)
            return remote(ref, ref, ds.at[0], dr.at[2], feat_sib)

        def receive():
            for part in range(2):
                @pl.when(core == part)
                def _():
                    end_differ(part).wait_recv()
                    share(part).start()

            end_sums().wait_recv()
            for part in range(2):
                @pl.when(core != part)
                def _():
                    share(part).wait_recv()

        def apply(src):
            loss_ref[...] += RL[1:2]
            rad_ref[...] += RL[0:1]
            g_ref[...] += jnp.dot(
                DE[...].reshape(n, n), X[src].reshape(n, w), preferred_element_type=F32
            )

        def scale():
            collect(squares_of, qs.at[0], qr.at[0])
            squares = SQ[0]
            for g in range(1, F):
                squares = squares + SQ[g]
            S[z] = lax.rsqrt(squares + EPSILON)
            s_copy(IN, z).start()
            if hub:
                s_copy(OUT, z).start()

        def teach_1():
            for place, src in enumerate((z, R - 1 - mate)):
                term = lax.dot_general(
                    T[src], T[mate], LAST, preferred_element_type=F32
                ).astype(BF16).reshape(NC, rc, n)
                for c in range(NC):
                    at = place * NC + c
                    TP[at // HC, at % HC] = term[c]
            for at in range(2 * NC, 2 * HC):
                TP[at // HC, at % HC] = jnp.zeros((rc, n), BF16)
            partial_out().start()

        def teach_2():
            partial_out().wait_recv()
            TE[...] = (TP[core].astype(F32) + TQ[...].astype(F32)).astype(BF16)
            end_part().start()

        def partial_out():
            return remote(TP.at[1 - core], TQ, ps.at[0], pr.at[0], feat_sib)

        def end_part():
            return remote(TE, TG.at[core], es.at[0], er.at[0], {"rows": mate})

        radial_of = lambda g: RX.at[g]
        spread(squares_of, qs.at[0], qr.at[0])
        t_copy(z).start()
        if hub:
            far, last = R - 1 - z, R - 1 - mate
            send(IN, z, 0)
            send(OUT, z, 0, 1, 2)
            send(IN, z, 1)
            scale()
            own = gram(z, 0)
            t_copy(mate).wait_recv()
            t_copy(mate).start()
            send(IN, z, 2)
            send(OUT, z, 3)
            relay(IN, mate, 0)
            relay(OUT, far, 0)
            relay(IN, mate, 1)
            relay(OUT, far, 1)
            send(OUT, z, 4)
            relay(IN, mate, 2)
            s_copy(IN, far).wait_recv()
            t_copy(far).wait_recv()
            t_copy(last).wait_recv()
            teach_1()
            s_copy(IN, mate).wait_recv()
            s_copy(IN, mate).start()
            relay(IN, mate, 3)
            relay(OUT, far, 2)
            relay(IN, mate, 4)
            send(IN, z, 3, 4)
            teach_2()
            relay(OUT, last, 0)
            second = gram(mate, 1)
            relay(OUT, last, 1)
            third = gram(far, 2, 0, 3)
            s_copy(IN, last).wait_recv()
            s_copy(OUT, last).start()
            relay(OUT, last, 2)
            fourth = [gram(last, 3, 0, 3, both=0)]
            relay(OUT, last, 3)
            finish(own, first=True)
            relay(OUT, last, 4)
            fourth.append(gram(last, 3, 3, 2, both=0))
            relay(OUT, far, 3)
            fifth = gram(far, 2, 3, 1, both=1)
            finish(fourth[0], deliver=True)
            relay(OUT, far, 4)
            sixth = gram(far, 2, 4, 1, both=1)
            finish(fourth[1], deliver=True)
            finish(second)
            finish(third)
            spread(radial_of, rs.at[0], rr.at[0])
            finish(fifth)
            finish(sixth)
        else:
            far, last = R - 1 - mate, R - 1 - z
            send(IN, z, 0, 1, 2)
            scale()
            send(IN, z, 3, 4)
            own = gram(z, 0)
            here(mate, 0, 1, 2, 3)
            here(far, 0, 1)
            here(mate, 4)
            finish(own, first=True)
            here(far, 2)
            s_copy(IN, mate).wait_recv()
            end_part().wait_recv()
            second = gram(mate, 1)
            here(last, 0, 1, 2)
            s_copy(IN, last).wait_recv()
            fourth = [gram(last, 2, 0, 3, both=0)]
            finish(second)
            spread(radial_of, rs.at[0], rr.at[0])
            here(last, 3, 4)
            fourth.append(gram(last, 2, 3, 2, both=0))
            here(far, 3)
            finish(fourth[0])
            receive()
            finish(fourth[1])
            here(far, 4)
            apply(far)
        collect(radial_of, rs.at[0], rr.at[0])
        for g in range(F):
            rad_ref[...] += RX[g, :1]

        drained(SQ.at[pl.ds(0, F - 1)], qs.at[0], qr.at[0])
        drained(CX.at[pl.ds(0, F - 1), pl.ds(0, R if hub else R - 1)], cs.at[0], cr.at[0])
        drained(CY.at[pl.ds(0, F - 1), 0], cs.at[1], cr.at[0])
        drained(RX.at[pl.ds(0, F - 1)], rs.at[0], rr.at[0])
        drained(T.at[pl.ds(0, 2 if hub else 1)], ts.at[0], tr.at[0])
        drained(X.at[pl.ds(0, 2 if hub else 1)], xs.at[IN], xr.at[0, 0])
        drained(S.at[pl.ds(0, 2 if hub else 1)], ss.at[IN], sr.at[0])
        for part in range(2):
            @pl.when(core == part)
            def _():
                (end_differ if hub else share)(part).wait_send()

        if hub:
            end_sums().wait_send()
            drained(CY.at[pl.ds(0, F - 1), 1, pl.ds(3, NC - 3)], cs.at[2], cr.at[0])
            drained(X.at[pl.ds(0, 3)], xs.at[OUT], xr.at[0, 0])
            drained(S.at[pl.ds(0, 2)], ss.at[OUT], sr.at[0])
            partial_out().wait_send()
            end_part().wait_send()

    @pl.when(is_hub)
    def _():
        program(True)

    @pl.when(is_end)
    def _():
        program(False)

    factor = 4.0 * D / (n * R)
    loss_ref[...] = (D / (n * R)) * loss_ref[...]
    scaling = to_column(S[z][:1])
    radial = to_column(rad_ref[...])
    g_ref[...] = (factor * scaling) * (g_ref[...] - (radial * scaling) * x_ref[...])


def fused(R, F, student, teacher):
    n, w = student.shape
    wt = teacher.shape[1]
    NC = n // CHUNK
    HC = NC
    dma = pltpu.SemaphoreType.DMA
    vmem = pl.BlockSpec(memory_space=pltpu.VMEM)
    hbm = pl.BlockSpec(memory_space=pltpu.HBM)
    loss, grad = pl.pallas_call(
        functools.partial(kernel, R, F, NC),
        out_shape=(
            jax.ShapeDtypeStruct((1, n), F32),
            jax.ShapeDtypeStruct((n, w), F32),
        ),
        in_specs=[hbm, hbm],
        out_specs=(vmem, vmem),
        scratch_shapes=[
            pltpu.VMEM((n, w), F32),
            pltpu.VMEM((R, NC, CHUNK, w), BF16),
            pltpu.VMEM((R, n, wt), BF16),
            pltpu.VMEM((F, 8, n), F32),
            pltpu.VMEM((R, 8, n), F32),
            pltpu.VMEM((F, R, NC, CHUNK, n), BF16),
            pltpu.VMEM((F, 2, NC, CHUNK, n), BF16),
            pltpu.VMEM((R, NC, CHUNK, n), F32),
            pltpu.VMEM((2, HC, CHUNK, n), BF16),
            pltpu.VMEM((HC, CHUNK, n), BF16),
            pltpu.VMEM((HC, CHUNK, n), BF16),
            pltpu.VMEM((2, HC, CHUNK, n), BF16),
            pltpu.VMEM((F, 8, n), F32),
            pltpu.VMEM((NC, CHUNK, n), BF16),
            pltpu.VMEM((8, n), F32),
            pltpu.VMEM((1, n), F32),
            dma((2,)),
            dma((2,)), dma((R, NC)),
            dma((1,)), dma((R,)),
            dma((2,)), dma((R,)),
            dma((1,)), dma((1,)),
            dma((3,)), dma((11,)),
            dma((1,)), dma((1,)), dma((1,)), dma((1,)), dma((1,)), dma((1,)),
            dma((2,)), dma((3,)),
        ],
        compiler_params=pltpu.CompilerParams(
            collective_id=0, has_side_effects=True, vmem_limit_bytes=48 * 2**20
        ),
    )(pltpu.with_memory_space_constraint(student, pltpu.HBM), pltpu.with_memory_space_constraint(teacher, pltpu.HBM))
    return loss.reshape(n), grad


def solution(mesh):
    R, F = mesh.shape["rows"], mesh.shape["feat"]
    body = functools.partial(fused, R, F) if R == 4 and F == 4 else ring
    in_specs = (P(("groups", "rows"), "feat"), P(("groups", "rows"), "feat"))
    out_specs = (P(("groups", "rows")), P(("groups", "rows"), "feat"))
    return jax.shard_map(
        body, mesh=mesh, in_specs=in_specs, out_specs=out_specs, check_vma=False
    )
```

```python
import functools

import jax
import jax.numpy as jnp
from jax import lax
from jax.experimental import pallas as pl
from jax.experimental.pallas import tpu as pltpu
from jax.sharding import PartitionSpec as P

D = 4096
EPSILON = 1e-06
CHUNK = 32
LANES = 128
LAST = (((1,), (1,)), ((), ()))
FIRST = (((0,), (0,)), ((), ()))
F32 = jnp.float32
BF16 = jnp.bfloat16
MESH = pl.DeviceIdType.MESH


def shifted(block, axis, distance):
    devices = range(lax.axis_size(axis))
    route = [((i - distance) % len(devices), i) for i in devices]
    return lax.ppermute(block, axis, route)


def ring(student, teacher):
    cycle = lax.axis_size("rows")
    rows_here = student.shape[0]
    width = student.shape[1]
    embeds = rows_here * cycle
    squares = lax.psum(jnp.sum(student * student, axis=1), "feat")
    scaling = lax.rsqrt(squares + EPSILON)
    unit = student * scaling[:, None]
    unit_half = unit.astype(BF16)
    packed = jnp.concatenate([unit_half, teacher], axis=1)

    def absorb(carry, visitor):
        losses, pulled = carry
        other_unit = visitor[:, :width]
        other_teacher = visitor[:, width:]
        student_term = lax.dot_general(
            unit_half, other_unit, LAST, preferred_element_type=F32
        )
        teacher_term = lax.dot_general(
            teacher, other_teacher, LAST, preferred_element_type=F32
        )
        differ = lax.psum((student_term - teacher_term).astype(BF16), "feat").astype(F32)
        losses = losses + jnp.sum(differ * differ, axis=1)
        pulled = pulled + jnp.dot(
            differ.astype(BF16), other_unit, preferred_element_type=F32
        )
        return (losses, pulled)

    carry = (jnp.zeros((rows_here,), F32), jnp.zeros((rows_here, width), F32))
    carry = absorb(carry, packed)

    def turn(step, state):
        inner, visitor = state
        visitor = shifted(visitor, "rows", 1)
        return (absorb(inner, visitor), visitor)

    carry, visitor = lax.fori_loop(0, cycle - 1, turn, (carry, packed))
    losses, pulled = carry
    radial = lax.psum(jnp.sum(pulled * unit, axis=1), "feat")
    factor = 4.0 * D / embeds
    student_grad = factor * scaling[:, None] * (pulled - radial[:, None] * unit)
    return (D / embeds * losses, student_grad)


def rows_of(m):
    return -(-(m + m // 4) // 16) * 16


def kernel(
    R, F, NC, x_hbm, t_hbm, loss_ref, g_ref,
    x_ref, X, T, SQ, S, CP, CQ, CS, DE, RL, RB, rad_ref,
    ins, xs, xr, ts, tr, ss, sr, qs, qr, ps, pr, cs, cr, ds, dr, ls, lr, hr, bs, br,
):
    z = lax.axis_index("rows")
    f = lax.axis_index("feat")
    core = lax.rem(f, 2)
    chip = lax.div(f, 2)
    n, w = x_ref.shape
    rc = n // NC
    RL[...] = jnp.zeros_like(RL)
    mate = z + 1 - 2 * lax.rem(z, 2)
    is_hub = jnp.logical_or(z == 1, z == 2)
    is_end = jnp.logical_not(is_hub)
    IN, OUT = 0, 1

    bar = pltpu.get_barrier_semaphore()
    for p in range(1, F):
        pl.semaphore_signal(
            bar, inc=1, device_id={"feat": lax.rem(f + p, F)}, device_id_type=MESH
        )
    pl.semaphore_signal(bar, inc=1, device_id={"rows": mate}, device_id_type=MESH)

    @pl.when(is_hub)
    def _():
        pl.semaphore_signal(bar, inc=1, device_id={"rows": R - 1 - z}, device_id_type=MESH)

    x_in = pltpu.make_async_copy(x_hbm, x_ref, ins.at[0])
    t_in = pltpu.make_async_copy(t_hbm, T.at[z], ins.at[1])
    x_in.start()
    t_in.start()

    eye = lax.broadcasted_iota(jnp.int32, (n, n), 0) == lax.broadcasted_iota(
        jnp.int32, (n, n), 1
    )

    def to_row(column):
        return jnp.sum(jnp.where(eye, column, 0.0), axis=0, keepdims=True)

    def to_column(row):
        return jnp.sum(jnp.where(eye, row, 0.0), axis=1, keepdims=True)

    x_in.wait()
    x = x_ref[...]
    X[z] = x.astype(BF16).reshape(NC, rc, w)
    SQ[f] = jnp.broadcast_to(to_row(jnp.sum(x * x, axis=1, keepdims=True)), (8, n))
    t_in.wait()
    pl.semaphore_wait(bar, F + is_hub.astype(jnp.int32))

    def pack(value):
        m = value.shape[0]
        q = m // 4
        rest = [value[i * q:(i + 1) * q, LANES:] for i in range(4)]
        return jnp.concatenate([value[:, :LANES], jnp.concatenate(rest, axis=1)], axis=0)

    def unpack(value, m):
        q = m // 4
        t = n - LANES
        rest = [value[m:m + q, i * t:(i + 1) * t] for i in range(4)]
        return jnp.concatenate([value[:m], jnp.concatenate(rest, axis=0)], axis=1)

    def remote(src, dst, send, recv, device):
        return pltpu.make_async_remote_copy(
            src_ref=src, dst_ref=dst, send_sem=send, recv_sem=recv,
            device_id=device, device_id_type=MESH,
        )

    def spread(ref_of, send, recv):
        for p in range(1, F):
            remote(
                ref_of(f), ref_of(f), send, recv, {"feat": lax.rem(f + p, F)}
            ).start()

    def collect(ref_of, send, recv):
        ref = ref_of(pl.ds(0, F - 1))
        remote(ref, ref, send, recv, feat_x).wait_recv()

    def drained(ref, send, recv):
        remote(ref, ref, send, recv, feat_x).wait_send()

    squares_of = lambda g: SQ.at[g]
    feat_x = {"feat": lax.rem(f + 2, F)}
    feat_sib = {"feat": f + 1 - 2 * core}
    feat_diag = {"feat": F - 1 - f}

    def program(hub):
        def device(d):
            if not hub or d == OUT:
                return {"rows": mate}
            return {"rows": R - 1 - z}

        def x_copy(d, src, c):
            ref = X.at[src, c]
            return remote(ref, ref, xs.at[d], xr.at[src, c], device(d))

        def t_copy(src):
            ref = T.at[src]
            return remote(ref, ref, ts.at[0], tr.at[src], device(IN))

        def s_copy(src):
            ref = S.at[src]
            return remote(ref, ref, ss.at[0], sr.at[src], device(IN))

        def send(d, src, *chunks):
            for c in chunks:
                x_copy(d, src, c).start()

        def here(src, *chunks):
            for c in chunks:
                x_copy(IN, src, c).wait_recv()

        def relay(d, src, c):
            here(src, c)
            send(d, src, c)

        pieces = []

        def spot(c, m):
            return lax.broadcasted_iota(jnp.int32, (m, n), 0) + c * rc == (
                lax.broadcasted_iota(jnp.int32, (m, n), 1)
            )

        def column_of(src, c, m):
            return jnp.sum(jnp.where(spot(c, m), S[src][:1], 0.0), axis=1, keepdims=True)

        def halve(slot):
            at = pieces[slot][0]
            return remote(CP.at[1 - core, at], CQ.at[at], ps.at[0], pr.at[slot], feat_sib)

        def whole(slot, to, kind):
            at = pieces[slot][0]
            ref = CS.at[chip, kind, at]
            return remote(
                ref, ref, cs.at[0 if to is feat_sib else 1], cr.at[slot], to
            )

        def gram(src, by, c=0, k=NC):
            m = k * rc
            cosine = lax.dot_general(
                X[src, pl.ds(c, k)].reshape(m, w), X[by].reshape(n, w),
                LAST, preferred_element_type=F32,
            )
            cosine = cosine * S[by][:1] * column_of(src, c, m)
            term = cosine - lax.dot_general(
                T[src, pl.ds(c * rc, m)], T[by], LAST, preferred_element_type=F32
            )
            slot = len(pieces)
            start = 0 if slot == 0 else pieces[-1][4]
            stop = start + rows_of(m)
            used = pl.ds(start, m + m // 4)
            pieces.append((pl.ds(start, stop - start), c, k, src, stop, used))
            CP[0, used] = pack(term).astype(BF16)
            CP[1, used] = pack(cosine).astype(BF16)
            halve(slot).start()
            return slot

        def push(*slots):
            for slot in slots:
                used = pieces[slot][5]
                halve(slot).wait_recv()
                CS[chip, core, used] = (
                    CP[core, used].astype(F32) + CQ[used].astype(F32)
                ).astype(BF16)

                @pl.when(core == 0)
                def _():
                    for to in (feat_x, feat_diag, feat_sib):
                        whole(slot, to, 0).start()

                @pl.when(core == 1)
                def _():
                    whole(slot, feat_x, 1).start()

        def arrive(slot):
            at = pieces[slot][0]

            @pl.when(core == 0)
            def _():
                ref = CS.at[0, 0, at]
                remote(ref, ref, cs.at[0], cr.at[slot], feat_x).wait_recv()

            @pl.when(core == 1)
            def _():
                size = pieces[slot][4] - pieces[slot][0].start
                ref = CP.at[0, pl.ds(0, 3 * size)]
                remote(ref, ref, cs.at[0], cr.at[slot], feat_x).wait_recv()

        def summed(slot, kind):
            used, m = pieces[slot][5], pieces[slot][2] * rc
            return unpack(CS[0, kind, used].astype(F32) + CS[1, kind, used].astype(F32), m)

        def deliver(q, c, k, half, loss):
            for part in range(2):
                lo, hi = (0, 3) if part == 0 else (3, NC)
                if c <= lo and hi <= c + k:
                    DE[q, used_of(part)] = pack(
                        half[(lo - c) * rc:(hi - c) * rc].astype(F32)
                    ).astype(BF16)

                    @pl.when(core == part)
                    def _():
                        end_differ(q, part).start()

            if c == 0:
                RL[q, 0:1] = loss
            else:
                RL[q, 0:1] += loss

        def finish(slot, first=False, to=None, mine=True):
            _, c, k, src, _, _ = pieces[slot]
            m = k * rc
            arrive(slot)
            differ = summed(slot, 0)
            column = column_of(src, c, m)
            squared = differ * differ
            half = differ * column

            def as_row(v):
                v = jnp.sum(v, axis=1, keepdims=True)
                return jnp.sum(jnp.where(spot(c, m), v, 0.0), axis=0, keepdims=True)

            if to is not None:
                if mine:
                    deliver(to, c, k, differ * S[z][:1], as_row(squared))
                else:
                    deliver(to, c, k, half, jnp.sum(squared, axis=0, keepdims=True))

            @pl.when(core == 1)
            def _():
                inner = differ * summed(slot, 1)
                radial = jnp.sum(inner, axis=0, keepdims=True)
                if mine:
                    if first:
                        rad_ref[...] = radial
                    else:
                        rad_ref[...] += radial
                if to is not None:
                    RL[to, 1:2] += as_row(inner) if mine else radial

            if to is not None and c + k == NC:
                end_sums(to).start()
            if not mine:
                return
            loss = jnp.sum(squared, axis=0, keepdims=True)
            pulled = lax.dot_general(
                half.astype(BF16), X[src, pl.ds(c, k)].reshape(m, w), FIRST,
                preferred_element_type=F32,
            )
            if first:
                loss_ref[...] = loss
                g_ref[...] = pulled
            else:
                loss_ref[...] += loss
                g_ref[...] += pulled

        def radial_out():
            return remote(RB, RB, bs.at[0], br.at[0], feat_sib)

        def settle():
            @pl.when(core == 1)
            def _():
                RB[...] = jnp.broadcast_to(rad_ref[...], (8, n))
                radial_out().start()

        def used_of(part):
            m = (3 if part == 0 else NC - 3) * rc
            return pl.ds(0 if part == 0 else rows_of(3 * rc), m + m // 4)

        def part_of(q, part):
            first = rows_of(3 * rc)
            if part == 0:
                return DE.at[q, pl.ds(0, first)]
            return DE.at[q, pl.ds(first, rows_of((NC - 3) * rc))]

        def end_of(q):
            return {"rows": mate if q < 2 else R - 1 - mate}

        def end_differ(q, part):
            ref = part_of(q, part)
            return remote(ref, ref, ds.at[q], dr.at[q], end_of(q))

        def end_sums(q):
            return remote(RL.at[q], RL.at[q], ls.at[0], lr.at[q], end_of(q))

        def share(q, part):
            ref = part_of(q, part)
            return remote(ref, ref, ds.at[q], hr.at[q], feat_sib)

        def receive(q):
            for part in range(2):
                @pl.when(core == part)
                def _():
                    end_differ(q, part).wait_recv()
                    share(q, part).start()

        def apply(q, src, last=False):
            end_sums(q).wait_recv()
            for part in range(2):
                @pl.when(core != part)
                def _():
                    share(q, part).wait_recv()

            loss_ref[...] += RL[q, 0:1]

            @pl.when(core == 1)
            def _():
                rad_ref[...] += RL[q, 1:2]

            half = jnp.concatenate([
                unpack(DE[q, used_of(part)].astype(F32), (3 if part == 0 else NC - 3) * rc)
                for part in range(2)
            ]).astype(BF16)
            if last:
                settle()
            g_ref[...] += lax.dot_general(
                half, X[src].reshape(n, w),
                FIRST if q == 1 else (((1,), (0,)), ((), ())), preferred_element_type=F32,
            )

        def scale():
            collect(squares_of, qs.at[0], qr.at[0])
            squares = SQ[0]
            for g in range(1, F):
                squares = squares + SQ[g]
            S[z] = lax.rsqrt(squares + EPSILON)
            s_copy(z).start()

        spread(squares_of, qs.at[0], qr.at[0])
        t_copy(z).start()
        if hub:
            far, last = R - 1 - z, R - 1 - mate
            send(IN, z, 0)
            send(OUT, z, 0, 1, 2)
            send(IN, z, 1)
            scale()
            own = gram(z, z)
            t_copy(mate).wait_recv()
            t_copy(mate).start()
            send(OUT, z, 3)
            relay(IN, mate, 0)
            relay(OUT, far, 0)
            push(own)
            relay(IN, mate, 1)
            relay(OUT, far, 1)
            send(OUT, z, 4)
            s_copy(mate).wait_recv()
            s_copy(mate).start()
            relay(IN, mate, 2)
            relay(IN, mate, 3)
            relay(OUT, last, 0)
            relay(IN, mate, 4)
            send(IN, z, 2, 3, 4)
            near = gram(mate, z)
            relay(OUT, last, 1)
            push(near)
            t_copy(far).wait_recv()
            t_copy(last).wait_recv()
            s_copy(far).wait_recv()
            relay(OUT, last, 2)
            relay(OUT, last, 3)
            s_copy(last).wait_recv()
            one = gram(last, z, 0, 3)
            two = gram(last, mate, 0, 3)
            relay(OUT, last, 4)
            push(one, two)
            three = gram(last, z, 3, 2)
            four = gram(last, mate, 3, 2)
            finish(own, first=True)
            relay(OUT, far, 2)
            push(three, four)
            finish(near, to=0)
            five = gram(far, z, 0, 3)
            relay(OUT, far, 3)
            push(five)
            finish(one, to=2)
            finish(two, to=1, mine=False)
            relay(OUT, far, 4)
            six = gram(far, z, 3, 2)
            push(six)
            finish(three, to=2)
            finish(four, to=1, mine=False)
            finish(five)
            finish(six)
            settle()
        else:
            far, last = R - 1 - mate, R - 1 - z
            send(IN, z, 0, 1)
            scale()
            send(IN, z, 2, 3, 4)
            own = gram(z, z)
            push(own)
            here(mate, 0, 1, 2, 3)
            here(far, 0, 1)
            here(mate, 4)
            finish(own, first=True)
            receive(0)
            here(last, 0, 1, 2, 3, 4)
            apply(0, mate)
            here(far, 2, 3)
            receive(1)
            receive(2)
            apply(1, last)
            here(far, 4)
            apply(2, far, last=True)

        drained(SQ.at[pl.ds(0, F - 1)], qs.at[0], qr.at[0])
        drained(T.at[pl.ds(0, 2 if hub else 1)], ts.at[0], tr.at[0])
        drained(X.at[pl.ds(0, 2 if hub else 1)], xs.at[IN], xr.at[0, 0])
        drained(S.at[pl.ds(0, 2 if hub else 1)], ss.at[0], sr.at[0])
        sent = pl.ds(0, pieces[-1][4])
        drained(CP.at[0, sent], ps.at[0], pr.at[0])

        @pl.when(core == 0)
        def _():
            drained(CS.at[0, 0, sent], cs.at[0], cr.at[0])
            drained(CS.at[0, pl.ds(0, 2), sent], cs.at[1], cr.at[0])
            radial_out().wait_recv()

        @pl.when(core == 1)
        def _():
            drained(CS.at[0, 0, sent], cs.at[1], cr.at[0])
            radial_out().wait_send()

        for q in range(3):
            for part in range(2):
                @pl.when(core == part)
                def _():
                    (end_differ if hub else share)(q, part).wait_send()

        if hub:
            drained(RL, ls.at[0], lr.at[0])
            drained(X.at[pl.ds(0, 3)], xs.at[OUT], xr.at[0, 0])

    @pl.when(is_hub)
    def _():
        program(True)

    @pl.when(is_end)
    def _():
        program(False)

    factor = 4.0 * D / (n * R)
    loss_ref[...] = (D / (n * R)) * loss_ref[...]
    scaling = to_column(S[z][:1])
    radial = to_column(RB[:1])
    g_ref[...] = (factor * scaling) * (g_ref[...] - (radial * scaling) * x_ref[...])


def fused(R, F, student, teacher):
    n, w = student.shape
    wt = teacher.shape[1]
    NC = n // CHUNK
    big, small = rows_of(3 * CHUNK), rows_of(n - 3 * CHUNK)
    total = 2 * rows_of(n) + 3 * (big + small)
    dma = pltpu.SemaphoreType.DMA
    vmem = pl.BlockSpec(memory_space=pltpu.VMEM)
    hbm = pl.BlockSpec(memory_space=pltpu.HBM)
    loss, grad = pl.pallas_call(
        functools.partial(kernel, R, F, NC),
        out_shape=(
            jax.ShapeDtypeStruct((1, n), F32),
            jax.ShapeDtypeStruct((n, w), F32),
        ),
        in_specs=[hbm, hbm],
        out_specs=(vmem, vmem),
        scratch_shapes=[
            pltpu.VMEM((n, w), F32),
            pltpu.VMEM((R, NC, CHUNK, w), BF16),
            pltpu.VMEM((R, n, wt), BF16),
            pltpu.VMEM((F, 8, n), F32),
            pltpu.VMEM((R, 8, n), F32),
            pltpu.VMEM((2, total, LANES), BF16),
            pltpu.VMEM((total, LANES), BF16),
            pltpu.VMEM((2, 2, total, LANES), BF16),
            pltpu.VMEM((3, rows_of(3 * CHUNK) + rows_of(n - 3 * CHUNK), LANES), BF16),
            pltpu.VMEM((3, 8, n), F32),
            pltpu.VMEM((8, n), F32),
            pltpu.VMEM((1, n), F32),
            dma((2,)),
            dma((2,)), dma((R, NC)),
            dma((1,)), dma((R,)),
            dma((1,)), dma((R,)),
            dma((1,)), dma((1,)),
            dma((1,)), dma((8,)), dma((2,)), dma((8,)),
            dma((3,)), dma((3,)), dma((1,)), dma((3,)), dma((3,)),
            dma((1,)), dma((1,)),
        ],
        compiler_params=pltpu.CompilerParams(
            collective_id=0, has_side_effects=True, vmem_limit_bytes=48 * 2**20
        ),
    )(pltpu.with_memory_space_constraint(student, pltpu.HBM), pltpu.with_memory_space_constraint(teacher, pltpu.HBM))
    return loss.reshape(n), grad


def solution(mesh):
    R, F = mesh.shape["rows"], mesh.shape["feat"]
    body = functools.partial(fused, R, F) if R == 4 and F == 4 else ring
    in_specs = (P(("groups", "rows"), "feat"), P(("groups", "rows"), "feat"))
    out_specs = (P(("groups", "rows")), P(("groups", "rows"), "feat"))
    return jax.shard_map(
        body, mesh=mesh, in_specs=in_specs, out_specs=out_specs, check_vma=False
    )
```

```python
import functools

import jax
import jax.numpy as jnp
from jax import lax
from jax.experimental import pallas as pl
from jax.experimental.pallas import tpu as pltpu
from jax.sharding import PartitionSpec as P

D = 4096
EPSILON = 1e-06
CHUNK = 32
LANES = 128
QUARTER = 32
LAST = (((1,), (1,)), ((), ()))
FIRST = (((0,), (0,)), ((), ()))
F32 = jnp.float32
BF16 = jnp.bfloat16
MESH = pl.DeviceIdType.MESH


def shifted(block, axis, distance):
    devices = range(lax.axis_size(axis))
    route = [((i - distance) % len(devices), i) for i in devices]
    return lax.ppermute(block, axis, route)


def ring(student, teacher):
    cycle = lax.axis_size("rows")
    rows_here = student.shape[0]
    width = student.shape[1]
    embeds = rows_here * cycle
    squares = lax.psum(jnp.sum(student * student, axis=1), "feat")
    scaling = lax.rsqrt(squares + EPSILON)
    unit = student * scaling[:, None]
    unit_half = unit.astype(BF16)
    packed = jnp.concatenate([unit_half, teacher], axis=1)

    def absorb(carry, visitor):
        losses, pulled = carry
        other_unit = visitor[:, :width]
        other_teacher = visitor[:, width:]
        student_term = lax.dot_general(
            unit_half, other_unit, LAST, preferred_element_type=F32
        )
        teacher_term = lax.dot_general(
            teacher, other_teacher, LAST, preferred_element_type=F32
        )
        differ = lax.psum((student_term - teacher_term).astype(BF16), "feat").astype(F32)
        losses = losses + jnp.sum(differ * differ, axis=1)
        pulled = pulled + jnp.dot(
            differ.astype(BF16), other_unit, preferred_element_type=F32
        )
        return (losses, pulled)

    carry = (jnp.zeros((rows_here,), F32), jnp.zeros((rows_here, width), F32))
    carry = absorb(carry, packed)

    def turn(step, state):
        inner, visitor = state
        visitor = shifted(visitor, "rows", 1)
        return (absorb(inner, visitor), visitor)

    carry, visitor = lax.fori_loop(0, cycle - 1, turn, (carry, packed))
    losses, pulled = carry
    radial = lax.psum(jnp.sum(pulled * unit, axis=1), "feat")
    factor = 4.0 * D / embeds
    student_grad = factor * scaling[:, None] * (pulled - radial[:, None] * unit)
    return (D / embeds * losses, student_grad)


def rows_of(m):
    return -(-(m + m // 4) // 16) * 16


def kernel(
    R, F, NC, x_hbm, t_hbm, loss_ref, g_ref,
    x_ref, X, T, SQ, S, CP, CQ, CS, DE, RL, RB, SB, HB, rad_ref,
    ins, xs, xr, ts, tr, ss, sr, qs, qr, ps, pr, cs, cr, ds, dr, ls, lr, hr, ks, bs, br,
):
    z = lax.axis_index("rows")
    f = lax.axis_index("feat")
    core = lax.rem(f, 2)
    chip = lax.div(f, 2)
    n, w = x_ref.shape
    rc = n // NC
    RL[...] = jnp.zeros_like(RL)
    mate = z + 1 - 2 * lax.rem(z, 2)
    is_hub = jnp.logical_or(z == 1, z == 2)
    is_end = jnp.logical_not(is_hub)
    IN, OUT = 0, 1

    bar = pltpu.get_barrier_semaphore()
    for p in range(1, F):
        pl.semaphore_signal(
            bar, inc=1, device_id={"feat": lax.rem(f + p, F)}, device_id_type=MESH
        )
    pl.semaphore_signal(bar, inc=1, device_id={"rows": mate}, device_id_type=MESH)

    @pl.when(is_hub)
    def _():
        pl.semaphore_signal(bar, inc=1, device_id={"rows": R - 1 - z}, device_id_type=MESH)

    x_in = pltpu.make_async_copy(x_hbm, x_ref, ins.at[0])
    t_in = pltpu.make_async_copy(t_hbm, T.at[z], ins.at[1])
    x_in.start()
    t_in.start()

    eye = lax.broadcasted_iota(jnp.int32, (n, n), 0) == lax.broadcasted_iota(
        jnp.int32, (n, n), 1
    )

    def to_row(column):
        return jnp.sum(jnp.where(eye, column, 0.0), axis=0, keepdims=True)

    def to_column(row):
        return jnp.sum(jnp.where(eye, row, 0.0), axis=1, keepdims=True)

    x_in.wait()
    x = x_ref[...]
    X[z] = x.astype(BF16).reshape(NC, rc, w)
    SQ[f] = jnp.broadcast_to(to_row(jnp.sum(x * x, axis=1, keepdims=True)), (8, n))
    t_in.wait()
    pl.semaphore_wait(bar, F + is_hub.astype(jnp.int32))

    def pack(value):
        m = value.shape[0]
        q = m // 4
        rest = [value[i * q:(i + 1) * q, LANES:] for i in range(4)]
        return jnp.concatenate([value[:, :LANES], jnp.concatenate(rest, axis=1)], axis=0)

    def unpack(value, m):
        q = m // 4
        t = n - LANES
        rest = [value[m:m + q, i * t:(i + 1) * t] for i in range(4)]
        return jnp.concatenate([value[:m], jnp.concatenate(rest, axis=0)], axis=1)

    def remote(src, dst, send, recv, device):
        return pltpu.make_async_remote_copy(
            src_ref=src, dst_ref=dst, send_sem=send, recv_sem=recv,
            device_id=device, device_id_type=MESH,
        )

    def spread(ref_of, send, recv):
        for p in range(1, F):
            remote(
                ref_of(f), ref_of(f), send, recv, {"feat": lax.rem(f + p, F)}
            ).start()

    def collect(ref_of, send, recv):
        ref = ref_of(pl.ds(0, F - 1))
        remote(ref, ref, send, recv, feat_x).wait_recv()

    def drained(ref, send, recv):
        remote(ref, ref, send, recv, feat_x).wait_send()

    squares_of = lambda g: SQ.at[g]
    feat_x = {"feat": lax.rem(f + 2, F)}
    feat_sib = {"feat": f + 1 - 2 * core}
    feat_diag = {"feat": F - 1 - f}

    def program(hub):
        def device(d):
            if not hub or d == OUT:
                return {"rows": mate}
            return {"rows": R - 1 - z}

        def x_copy(d, src, c):
            ref = X.at[src, c]
            return remote(ref, ref, xs.at[d], xr.at[src, c], device(d))

        def t_copy(src):
            ref = T.at[src]
            return remote(ref, ref, ts.at[0], tr.at[src], device(IN))

        def s_copy(src):
            ref = S.at[src]
            return remote(ref, ref, ss.at[0], sr.at[src], device(IN))

        def send(d, src, *chunks):
            for c in chunks:
                x_copy(d, src, c).start()

        def here(src, *chunks):
            for c in chunks:
                x_copy(IN, src, c).wait_recv()

        def relay(d, src, c):
            here(src, c)
            send(d, src, c)

        pieces = []

        def spot(c, m):
            return lax.broadcasted_iota(jnp.int32, (m, n), 0) + c * rc == (
                lax.broadcasted_iota(jnp.int32, (m, n), 1)
            )

        def widen(src):
            column = jnp.sum(jnp.where(spot(0, n), S[src][:1], 0.0), axis=1, keepdims=True)
            SB[src] = jnp.broadcast_to(column, (n, n))

        def column_of(src, c, m):
            return SB[src, pl.ds(c * rc, m)]

        def halve(slot):
            at = pieces[slot][0]
            return remote(CP.at[1 - core, at], CQ.at[at], ps.at[0], pr.at[slot], feat_sib)

        def whole(slot, to, kind):
            at = pieces[slot][0]
            ref = CS.at[chip, kind, at]
            return remote(
                ref, ref, cs.at[0 if to is feat_sib else 1], cr.at[slot], to
            )

        def gram(src, by, c=0, k=NC):
            m = k * rc
            cosine = lax.dot_general(
                X[src, pl.ds(c, k)].reshape(m, w), X[by].reshape(n, w),
                LAST, preferred_element_type=F32,
            )
            cosine = cosine * S[by][:1] * column_of(src, c, m)
            term = cosine - lax.dot_general(
                T[src, pl.ds(c * rc, m)], T[by], LAST, preferred_element_type=F32
            )
            slot = len(pieces)
            start = 0 if slot == 0 else pieces[-1][4]
            stop = start + rows_of(m)
            used = pl.ds(start, m + m // 4)
            pieces.append((pl.ds(start, stop - start), c, k, src, stop, used))
            CP[0, used] = pack(term).astype(BF16)
            CP[1, used] = pack(cosine).astype(BF16)
            halve(slot).start()
            return slot

        def push(*slots):
            for slot in slots:
                used = pieces[slot][5]
                halve(slot).wait_recv()
                CS[chip, core, used] = (
                    CP[core, used].astype(F32) + CQ[used].astype(F32)
                ).astype(BF16)

                @pl.when(core == 0)
                def _():
                    for to in (feat_x, feat_diag, feat_sib):
                        whole(slot, to, 0).start()

                @pl.when(core == 1)
                def _():
                    whole(slot, feat_x, 1).start()

        def arrive(slot):
            at = pieces[slot][0]

            @pl.when(core == 0)
            def _():
                ref = CS.at[0, 0, at]
                remote(ref, ref, cs.at[0], cr.at[slot], feat_x).wait_recv()

            @pl.when(core == 1)
            def _():
                size = pieces[slot][4] - pieces[slot][0].start
                ref = CP.at[0, pl.ds(0, 3 * size)]
                remote(ref, ref, cs.at[0], cr.at[slot], feat_x).wait_recv()

        def summed(slot, kind):
            used, m = pieces[slot][5], pieces[slot][2] * rc
            return unpack(CS[0, kind, used].astype(F32) + CS[1, kind, used].astype(F32), m)

        def deliver(q, c, k, half):
            for part, (lo, hi) in enumerate(((0, 3), (3, NC))):
                if c <= lo and hi <= c + k:
                    def fill():
                        DE[q, part, used_of(part)] = pack(
                            half()[(lo - c) * rc:(hi - c) * rc]
                        ).astype(BF16)
                        (end_half if q else end_differ)(q, part).start()

                    if q:
                        pl.when(core == part)(fill)
                    else:
                        fill()

        def finish(slot, to=None, mine=True, later=False):
            _, c, k, src, _, _ = pieces[slot]
            m = k * rc
            arrive(slot)
            differ = summed(slot, 0)
            if to is not None:
                deliver(
                    to, c, k,
                    lambda: differ * (S[z][:1] if mine else column_of(src, c, m)),
                )
            if mine:
                HB[src, pl.ds(c * rc, m)] = (differ * column_of(src, c, m)).astype(BF16)
            if not later:
                sums(slot, to, mine)

        def sums(slot, to=None, mine=True):
            _, c, k, src, _, _ = pieces[slot]
            m = k * rc

            @pl.when(core == 1)
            def _():
                differ = summed(slot, 0)
                squared = differ * differ
                inner = differ * summed(slot, 1)
                loss = jnp.sum(squared, axis=0, keepdims=True)
                radial = jnp.sum(inner, axis=0, keepdims=True)
                if mine and slot == 0:
                    rad_ref[...] = radial
                    loss_ref[...] = loss
                elif mine:
                    rad_ref[...] += radial
                    loss_ref[...] += loss
                if to is not None:
                    if mine:
                        loss, radial = (
                            jnp.sum(
                                jnp.where(spot(c, m), jnp.sum(v, axis=1, keepdims=True), 0.0),
                                axis=0, keepdims=True,
                            )
                            for v in (squared, inner)
                        )
                    RL[to // 2, 0:1] += radial
                    RL[to // 2, 1:2] += loss
                    if to > 0 and c + k == NC:
                        end_sums(to // 2).start()

        def radial_out():
            return remote(RB, RB, bs.at[0], br.at[0], feat_sib)

        def settle():
            @pl.when(core == 1)
            def _():
                RB[0:1] = rad_ref[...]
                RB[1:2] = loss_ref[...]
                radial_out().start()

        def used_of(part):
            m = (3 if part == 0 else NC - 3) * rc
            return pl.ds(0, m + m // 4)

        def end_of(q):
            return {"rows": mate if q < 2 else R - 1 - mate}

        def quarter(q, part, g):
            return DE.at[q, part, pl.ds(pl.multiple_of(g * QUARTER, QUARTER), QUARTER)]

        def end_differ(q, part):
            ref = quarter(q, part, f)
            return remote(ref, ref, ds.at[0], dr.at[2 * q + part], end_of(q))

        def end_sums(q):
            return remote(RL.at[q], RL.at[q], ls.at[q], lr.at[q], end_of(2 * q))

        def half_of(q, part):
            return DE.at[q, part, pl.ds(0, rows_of((3 if part == 0 else NC - 3) * rc))]

        def end_half(q, part):
            ref = half_of(q, part)
            return remote(ref, ref, ks.at[q - 1], dr.at[2 * q + part], end_of(q))

        def share(q, part):
            ref = half_of(q, part)
            return remote(ref, ref, ks.at[q - 1], hr.at[2 * q + part], feat_sib)

        def receive(q, part):
            if q:
                @pl.when(core == part)
                def _():
                    end_half(q, part).wait_recv()
                    share(q, part).start()

                return
            end_differ(q, part).wait_recv()
            spread(lambda g: quarter(q, part, g), ds.at[0], hr.at[2 * q + part])

        def apply(q, src, last=False):
            for part in range(2 if q else 0):
                @pl.when(core != part)
                def _():
                    share(q, part).wait_recv()

            for part in range(0 if q else 2):
                ref = DE.at[q, part, pl.ds(0, (F - 1) * QUARTER)]
                remote(ref, ref, ds.at[0], hr.at[2 * q + part], feat_x).wait_recv()
            if last:
                @pl.when(core == 1)
                def _():
                    for side in range(2):
                        end_sums(side).wait_recv()
                        rad_ref[...] += RL[side, 0:1]
                        loss_ref[...] += RL[side, 1:2]

                settle()
            half = jnp.concatenate([
                unpack(DE[q, part, used_of(part)].astype(F32), (3 if part == 0 else NC - 3) * rc)
                for part in range(2)
            ]).astype(BF16)
            g_ref[...] += lax.dot_general(
                half, X[src].reshape(n, w),
                FIRST if q == 1 else (((1,), (0,)), ((), ())), preferred_element_type=F32,
            )

        def scale():
            collect(squares_of, qs.at[0], qr.at[0])
            squares = SQ[0]
            for g in range(1, F):
                squares = squares + SQ[g]
            S[z] = lax.rsqrt(squares + EPSILON)
            s_copy(z).start()
            widen(z)

        spread(squares_of, qs.at[0], qr.at[0])
        if hub:
            far, last = R - 1 - z, R - 1 - mate
            t_copy(z).start()
            send(IN, z, 0)
            send(OUT, z, 0, 1, 2)
            send(IN, z, 1)
            scale()
            own = gram(z, z)
            relay(IN, mate, 0)
            send(OUT, z, 3)
            relay(IN, mate, 1)
            relay(OUT, far, 0)
            push(own)
            relay(IN, mate, 2)
            s_copy(mate).wait_recv()
            s_copy(mate).start()
            widen(mate)
            relay(OUT, far, 1)
            t_copy(mate).wait_recv()
            t_copy(mate).start()
            relay(OUT, last, 0)
            relay(IN, mate, 3)
            relay(OUT, last, 1)
            relay(IN, mate, 4)
            send(IN, z, 2, 3, 4)
            relay(OUT, last, 2)
            send(OUT, z, 4)
            near = gram(mate, z)
            finish(own)
            push(near)
            s_copy(far).wait_recv()
            s_copy(last).wait_recv()
            widen(far)
            widen(last)
            t_copy(far).wait_recv()
            t_copy(last).wait_recv()
            one = gram(last, z, 0, 3)
            two = gram(last, mate, 0, 3)
            relay(OUT, last, 3)
            push(one, two)
            relay(OUT, last, 4)
            three = gram(last, z, 3, 2)
            four = gram(last, mate, 3, 2)
            finish(near, to=0)
            push(three, four)
            relay(OUT, far, 2)
            five = gram(far, z, 0, 3)
            relay(OUT, far, 3)
            push(five)
            finish(one, to=2)
            finish(two, to=1, mine=False)
            finish(four, to=1, mine=False, later=True)
            finish(three, to=2, later=True)
            relay(OUT, far, 4)
            six = gram(far, z, 3, 2)
            push(six)
            sums(three, to=2)
            sums(four, to=1, mine=False)
            finish(five)
            finish(six)
            settle()
            g_ref[...] = lax.dot_general(
                HB[...].reshape(R * n, n), X[...].reshape(R * n, w), FIRST,
                preferred_element_type=F32,
            )
        else:
            far, last = R - 1 - mate, R - 1 - z
            send(IN, z, 0, 1, 2)
            scale()
            t_copy(z).start()
            send(IN, z, 3, 4)
            own = gram(z, z)
            push(own)
            here(mate, 0, 1, 2, 3)
            here(far, 0, 1)
            here(last, 0, 1, 2)
            finish(own)
            g_ref[...] = lax.dot_general(
                HB[z], X[z].reshape(n, w), FIRST, preferred_element_type=F32
            )
            here(mate, 4)
            here(last, 3, 4)
            receive(0, 0)
            receive(0, 1)
            here(far, 2)
            receive(2, 0)
            receive(1, 0)
            here(far, 3)
            apply(0, mate)
            receive(2, 1)
            receive(1, 1)
            apply(1, last)
            here(far, 4)
            apply(2, far, last=True)

        drained(SQ.at[pl.ds(0, F - 1)], qs.at[0], qr.at[0])
        drained(T.at[pl.ds(0, 2 if hub else 1)], ts.at[0], tr.at[0])
        drained(X.at[pl.ds(0, 2 if hub else 1)], xs.at[IN], xr.at[0, 0])
        drained(S.at[pl.ds(0, 2 if hub else 1)], ss.at[0], sr.at[0])
        sent = pl.ds(0, pieces[-1][4])
        drained(CP.at[0, sent], ps.at[0], pr.at[0])

        @pl.when(core == 0)
        def _():
            drained(CS.at[0, 0, sent], cs.at[0], cr.at[0])
            drained(CS.at[0, pl.ds(0, 2), sent], cs.at[1], cr.at[0])
            radial_out().wait_recv()

        @pl.when(core == 1)
        def _():
            drained(CS.at[0, 0, sent], cs.at[1], cr.at[0])
            radial_out().wait_send()

        rows = 2 * QUARTER * (1 if hub else F - 1)
        drained(CP.at[0, pl.ds(0, rows)], ds.at[0], dr.at[0])
        for part in range(2):
            @pl.when(core == part)
            def _():
                for q in range(1, 3):
                    share(q, part).wait_send()


        if hub:
            @pl.when(core == 1)
            def _():
                for q in range(2):
                    end_sums(q).wait_send()

            drained(X.at[pl.ds(0, 3)], xs.at[OUT], xr.at[0, 0])

    @pl.when(is_hub)
    def _():
        program(True)

    @pl.when(is_end)
    def _():
        program(False)

    factor = 4.0 * D / (n * R)
    loss_ref[...] = (D / (n * R)) * RB[1:2]
    scaling = to_column(S[z][:1])
    radial = to_column(RB[:1])
    g_ref[...] = (factor * scaling) * (g_ref[...] - (radial * scaling) * x_ref[...])


def fused(R, F, student, teacher):
    n, w = student.shape
    wt = teacher.shape[1]
    NC = n // CHUNK
    big, small = rows_of(3 * CHUNK), rows_of(n - 3 * CHUNK)
    total = 2 * rows_of(n) + 3 * (big + small)
    dma = pltpu.SemaphoreType.DMA
    vmem = pl.BlockSpec(memory_space=pltpu.VMEM)
    hbm = pl.BlockSpec(memory_space=pltpu.HBM)
    loss, grad = pl.pallas_call(
        functools.partial(kernel, R, F, NC),
        out_shape=(
            jax.ShapeDtypeStruct((1, n), F32),
            jax.ShapeDtypeStruct((n, w), F32),
        ),
        in_specs=[hbm, hbm],
        out_specs=(vmem, vmem),
        scratch_shapes=[
            pltpu.VMEM((n, w), F32),
            pltpu.VMEM((R, NC, CHUNK, w), BF16),
            pltpu.VMEM((R, n, wt), BF16),
            pltpu.VMEM((F, 8, n), F32),
            pltpu.VMEM((R, 8, n), F32),
            pltpu.VMEM((2, total, LANES), BF16),
            pltpu.VMEM((total, LANES), BF16),
            pltpu.VMEM((2, 2, total, LANES), BF16),
            pltpu.VMEM((3, 2, F * QUARTER, LANES), BF16),
            pltpu.VMEM((2, 8, n), F32),
            pltpu.VMEM((8, n), F32),
            pltpu.VMEM((R, n, n), F32),
            pltpu.VMEM((R, n, n), BF16),
            pltpu.VMEM((1, n), F32),
            dma((2,)),
            dma((2,)), dma((R, NC)),
            dma((1,)), dma((R,)),
            dma((1,)), dma((R,)),
            dma((1,)), dma((1,)),
            dma((1,)), dma((8,)), dma((2,)), dma((8,)),
            dma((1,)), dma((6,)), dma((2,)), dma((2,)), dma((6,)), dma((2,)),
            dma((1,)), dma((1,)),
        ],
        compiler_params=pltpu.CompilerParams(
            collective_id=0, has_side_effects=True, vmem_limit_bytes=48 * 2**20
        ),
    )(pltpu.with_memory_space_constraint(student, pltpu.HBM), pltpu.with_memory_space_constraint(teacher, pltpu.HBM))
    return loss.reshape(n), grad


def solution(mesh):
    R, F = mesh.shape["rows"], mesh.shape["feat"]
    body = functools.partial(fused, R, F) if R == 4 and F == 4 else ring
    in_specs = (P(("groups", "rows"), "feat"), P(("groups", "rows"), "feat"))
    out_specs = (P(("groups", "rows")), P(("groups", "rows"), "feat"))
    return jax.shard_map(
        body, mesh=mesh, in_specs=in_specs, out_specs=out_specs, check_vma=False
    )
```

```python
import functools

import jax
import jax.numpy as jnp
from jax import lax
from jax.experimental import pallas as pl
from jax.experimental.pallas import tpu as pltpu
from jax.sharding import PartitionSpec as P

D = 4096
EPSILON = 1e-06
CHUNK = 32
LANES = 128
QUARTER = 32
LAST = (((1,), (1,)), ((), ()))
FIRST = (((0,), (0,)), ((), ()))
F32 = jnp.float32
BF16 = jnp.bfloat16
MESH = pl.DeviceIdType.MESH


def shifted(block, axis, distance):
    devices = range(lax.axis_size(axis))
    route = [((i - distance) % len(devices), i) for i in devices]
    return lax.ppermute(block, axis, route)


def ring(student, teacher):
    cycle = lax.axis_size("rows")
    rows_here = student.shape[0]
    width = student.shape[1]
    embeds = rows_here * cycle
    squares = lax.psum(jnp.sum(student * student, axis=1), "feat")
    scaling = lax.rsqrt(squares + EPSILON)
    unit = student * scaling[:, None]
    unit_half = unit.astype(BF16)
    packed = jnp.concatenate([unit_half, teacher], axis=1)

    def absorb(carry, visitor):
        losses, pulled = carry
        other_unit = visitor[:, :width]
        other_teacher = visitor[:, width:]
        student_term = lax.dot_general(
            unit_half, other_unit, LAST, preferred_element_type=F32
        )
        teacher_term = lax.dot_general(
            teacher, other_teacher, LAST, preferred_element_type=F32
        )
        differ = lax.psum((student_term - teacher_term).astype(BF16), "feat").astype(F32)
        losses = losses + jnp.sum(differ * differ, axis=1)
        pulled = pulled + jnp.dot(
            differ.astype(BF16), other_unit, preferred_element_type=F32
        )
        return (losses, pulled)

    carry = (jnp.zeros((rows_here,), F32), jnp.zeros((rows_here, width), F32))
    carry = absorb(carry, packed)

    def turn(step, state):
        inner, visitor = state
        visitor = shifted(visitor, "rows", 1)
        return (absorb(inner, visitor), visitor)

    carry, visitor = lax.fori_loop(0, cycle - 1, turn, (carry, packed))
    losses, pulled = carry
    radial = lax.psum(jnp.sum(pulled * unit, axis=1), "feat")
    factor = 4.0 * D / embeds
    student_grad = factor * scaling[:, None] * (pulled - radial[:, None] * unit)
    return (D / embeds * losses, student_grad)


def rows_of(m):
    return -(-(m + m // 4) // 16) * 16


def kernel(
    R, F, NC, x_hbm, t_hbm, loss_ref, g_ref,
    x_ref, X, T, SQ, S, CP, CQ, CS, DE, RL, RB, SB, HB, rad_ref,
    ins, xs, xr, ts, tr, ss, sr, qs, qr, ps, pr, cs, cr, ds, dr, ls, lr, hr, ks, bs, br,
):
    z = lax.axis_index("rows")
    f = lax.axis_index("feat")
    core = lax.rem(f, 2)
    chip = lax.div(f, 2)
    n, w = x_ref.shape
    rc = n // NC
    RL[...] = jnp.zeros_like(RL)
    mate = z + 1 - 2 * lax.rem(z, 2)
    is_hub = jnp.logical_or(z == 1, z == 2)
    is_end = jnp.logical_not(is_hub)
    IN, OUT = 0, 1

    bar = pltpu.get_barrier_semaphore()
    for p in range(1, F):
        pl.semaphore_signal(
            bar, inc=1, device_id={"feat": lax.rem(f + p, F)}, device_id_type=MESH
        )
    pl.semaphore_signal(bar, inc=1, device_id={"rows": mate}, device_id_type=MESH)

    @pl.when(is_hub)
    def _():
        pl.semaphore_signal(bar, inc=1, device_id={"rows": R - 1 - z}, device_id_type=MESH)

    x_in = pltpu.make_async_copy(x_hbm, x_ref, ins.at[0])
    t_in = pltpu.make_async_copy(t_hbm, T.at[z], ins.at[1])
    x_in.start()
    t_in.start()

    eye = lax.broadcasted_iota(jnp.int32, (n, n), 0) == lax.broadcasted_iota(
        jnp.int32, (n, n), 1
    )

    def to_row(column):
        return jnp.sum(jnp.where(eye, column, 0.0), axis=0, keepdims=True)

    def to_column(row):
        return jnp.sum(jnp.where(eye, row, 0.0), axis=1, keepdims=True)

    x_in.wait()
    x = x_ref[...]
    X[z] = x.astype(BF16).reshape(NC, rc, w)
    SQ[f] = jnp.broadcast_to(to_row(jnp.sum(x * x, axis=1, keepdims=True)), (8, n))
    t_in.wait()
    pl.semaphore_wait(bar, F + is_hub.astype(jnp.int32))

    def pack(value):
        m = value.shape[0]
        q = m // 4
        rest = [value[i * q:(i + 1) * q, LANES:] for i in range(4)]
        return jnp.concatenate([value[:, :LANES], jnp.concatenate(rest, axis=1)], axis=0)

    def unpack(value, m):
        q = m // 4
        t = n - LANES
        rest = [value[m:m + q, i * t:(i + 1) * t] for i in range(4)]
        return jnp.concatenate([value[:m], jnp.concatenate(rest, axis=0)], axis=1)

    def remote(src, dst, send, recv, device):
        return pltpu.make_async_remote_copy(
            src_ref=src, dst_ref=dst, send_sem=send, recv_sem=recv,
            device_id=device, device_id_type=MESH,
        )

    def spread(ref_of, send, recv):
        for p in range(1, F):
            remote(
                ref_of(f), ref_of(f), send, recv, {"feat": lax.rem(f + p, F)}
            ).start()

    def collect(ref_of, send, recv):
        ref = ref_of(pl.ds(0, F - 1))
        remote(ref, ref, send, recv, feat_x).wait_recv()

    def drained(ref, send, recv):
        remote(ref, ref, send, recv, feat_x).wait_send()

    squares_of = lambda g: SQ.at[g]
    feat_x = {"feat": lax.rem(f + 2, F)}
    feat_sib = {"feat": f + 1 - 2 * core}
    feat_diag = {"feat": F - 1 - f}

    def program(hub):
        def device(d):
            if not hub or d == OUT:
                return {"rows": mate}
            return {"rows": R - 1 - z}

        def x_copy(d, src, c):
            ref = X.at[src, c]
            return remote(ref, ref, xs.at[d], xr.at[src, c], device(d))

        def t_copy(src):
            ref = T.at[src]
            return remote(ref, ref, ts.at[0], tr.at[src], device(IN))

        def s_copy(src):
            ref = S.at[src]
            return remote(ref, ref, ss.at[0], sr.at[src], device(IN))

        def send(d, src, *chunks):
            for c in chunks:
                x_copy(d, src, c).start()

        def here(src, *chunks):
            for c in chunks:
                x_copy(IN, src, c).wait_recv()

        def relay(d, src, c):
            here(src, c)
            send(d, src, c)

        pieces = []

        def spot(c, m):
            return lax.broadcasted_iota(jnp.int32, (m, n), 0) + c * rc == (
                lax.broadcasted_iota(jnp.int32, (m, n), 1)
            )

        def widen(src):
            column = jnp.sum(jnp.where(spot(0, n), S[src][:1], 0.0), axis=1, keepdims=True)
            SB[src] = jnp.broadcast_to(column, (n, n))

        def column_of(src, c, m):
            return SB[src, pl.ds(c * rc, m)]

        def halve(slot):
            at = pieces[slot][0]
            return remote(CP.at[1 - core, at], CQ.at[at], ps.at[0], pr.at[slot], feat_sib)

        def whole(slot, to, kind):
            at = pieces[slot][0]
            ref = CS.at[chip, kind, at]
            return remote(
                ref, ref, cs.at[0 if to is feat_sib else 1], cr.at[slot], to
            )

        def gram(src, by, c=0, k=NC):
            m = k * rc
            cosine = lax.dot_general(
                X[src, pl.ds(c, k)].reshape(m, w), X[by].reshape(n, w),
                LAST, preferred_element_type=F32,
            )
            cosine = cosine * S[by][:1] * column_of(src, c, m)
            term = cosine - lax.dot_general(
                T[src, pl.ds(c * rc, m)], T[by], LAST, preferred_element_type=F32
            )
            slot = len(pieces)
            start = 0 if slot == 0 else pieces[-1][4]
            stop = start + rows_of(m)
            used = pl.ds(start, m + m // 4)
            pieces.append((pl.ds(start, stop - start), c, k, src, stop, used))
            CP[0, used] = pack(term).astype(BF16)
            CP[1, used] = pack(cosine).astype(BF16)
            halve(slot).start()
            return slot

        def push(*slots):
            for slot in slots:
                used = pieces[slot][5]
                halve(slot).wait_recv()
                CS[chip, core, used] = (
                    CP[core, used].astype(F32) + CQ[used].astype(F32)
                ).astype(BF16)

                @pl.when(core == 0)
                def _():
                    for to in (feat_x, feat_diag, feat_sib):
                        whole(slot, to, 0).start()

                @pl.when(core == 1)
                def _():
                    whole(slot, feat_x, 1).start()

        def arrive(slot):
            at = pieces[slot][0]

            @pl.when(core == 0)
            def _():
                ref = CS.at[0, 0, at]
                remote(ref, ref, cs.at[0], cr.at[slot], feat_x).wait_recv()

            @pl.when(core == 1)
            def _():
                size = pieces[slot][4] - pieces[slot][0].start
                ref = CP.at[0, pl.ds(0, 3 * size)]
                remote(ref, ref, cs.at[0], cr.at[slot], feat_x).wait_recv()

        def summed(slot, kind):
            used, m = pieces[slot][5], pieces[slot][2] * rc
            return unpack(CS[0, kind, used].astype(F32) + CS[1, kind, used].astype(F32), m)

        def deliver(q, c, k, half):
            for part, (lo, hi) in enumerate(((0, 3), (3, NC))):
                if c <= lo and hi <= c + k:
                    def fill():
                        DE[q, part, used_of(part)] = pack(
                            half()[(lo - c) * rc:(hi - c) * rc]
                        ).astype(BF16)
                        (end_half if q else end_differ)(q, part).start()

                    if q:
                        pl.when(core == part)(fill)
                    else:
                        fill()

        def finish(slot, to=None, mine=True, later=False):
            _, c, k, src, _, _ = pieces[slot]
            m = k * rc
            arrive(slot)
            differ = summed(slot, 0)
            if to is not None:
                deliver(
                    to, c, k,
                    lambda: differ * (S[z][:1] if mine else column_of(src, c, m)),
                )
            if mine:
                HB[src, pl.ds(c * rc, m)] = (differ * column_of(src, c, m)).astype(BF16)
            if not later:
                sums(slot, to, mine)

        def sums(slot, to=None, mine=True):
            _, c, k, src, _, _ = pieces[slot]
            m = k * rc

            @pl.when(core == 1)
            def _():
                differ = summed(slot, 0)
                squared = differ * differ
                inner = differ * summed(slot, 1)
                loss = jnp.sum(squared, axis=0, keepdims=True)
                radial = jnp.sum(inner, axis=0, keepdims=True)
                if mine and slot == 0:
                    rad_ref[...] = radial
                    loss_ref[...] = loss
                elif mine:
                    rad_ref[...] += radial
                    loss_ref[...] += loss
                if to is not None:
                    if mine:
                        loss, radial = (
                            jnp.sum(
                                jnp.where(spot(c, m), jnp.sum(v, axis=1, keepdims=True), 0.0),
                                axis=0, keepdims=True,
                            )
                            for v in (squared, inner)
                        )
                    RL[to // 2, 0:1] += radial
                    RL[to // 2, 1:2] += loss
                    if to > 0 and c + k == NC:
                        end_sums(to // 2).start()

        def radial_out():
            return remote(RB, RB, bs.at[0], br.at[0], feat_sib)

        def settle():
            @pl.when(core == 1)
            def _():
                RB[0:1] = rad_ref[...]
                RB[1:2] = loss_ref[...]
                radial_out().start()

        def used_of(part):
            m = (3 if part == 0 else NC - 3) * rc
            return pl.ds(0, m + m // 4)

        def end_of(q):
            return {"rows": mate if q < 2 else R - 1 - mate}

        def quarter(q, part, g):
            return DE.at[q, part, pl.ds(pl.multiple_of(g * QUARTER, QUARTER), QUARTER)]

        def end_differ(q, part):
            ref = quarter(q, part, f)
            return remote(ref, ref, ds.at[0], dr.at[2 * q + part], end_of(q))

        def end_sums(q):
            return remote(RL.at[q], RL.at[q], ls.at[q], lr.at[q], end_of(2 * q))

        def half_of(q, part):
            return DE.at[q, part, pl.ds(0, rows_of((3 if part == 0 else NC - 3) * rc))]

        def end_half(q, part):
            ref = half_of(q, part)
            return remote(ref, ref, ks.at[q - 1], dr.at[2 * q + part], end_of(q))

        def share(q, part):
            ref = half_of(q, part)
            return remote(ref, ref, ks.at[q - 1], hr.at[2 * q + part], feat_sib)

        def receive(q, part):
            if q:
                @pl.when(core == part)
                def _():
                    end_half(q, part).wait_recv()
                    share(q, part).start()

                return
            end_differ(q, part).wait_recv()
            spread(lambda g: quarter(q, part, g), ds.at[0], hr.at[2 * q + part])

        def totals():
            @pl.when(core == 1)
            def _():
                for side in range(2):
                    end_sums(side).wait_recv()
                    rad_ref[...] += RL[side, 0:1]
                    loss_ref[...] += RL[side, 1:2]

            settle()

        def apply(q, src):
            for part in range(2 if q else 0):
                @pl.when(core != part)
                def _():
                    share(q, part).wait_recv()

            for part in range(0 if q else 2):
                ref = DE.at[q, part, pl.ds(0, (F - 1) * QUARTER)]
                remote(ref, ref, ds.at[0], hr.at[2 * q + part], feat_x).wait_recv()
            half = jnp.concatenate([
                unpack(DE[q, part, used_of(part)].astype(F32), (3 if part == 0 else NC - 3) * rc)
                for part in range(2)
            ]).astype(BF16)
            if q == 2:
                early = (NC - 1) * rc
                g_ref[...] += jnp.dot(
                    half[:, :early], X[src, pl.ds(0, NC - 1)].reshape(early, w),
                    preferred_element_type=F32,
                )
                here(src, NC - 1)
                g_ref[...] += jnp.dot(
                    half[:, early:], X[src, NC - 1], preferred_element_type=F32
                )
                return
            g_ref[...] += lax.dot_general(
                half, X[src].reshape(n, w),
                FIRST if q == 1 else (((1,), (0,)), ((), ())), preferred_element_type=F32,
            )

        def scale():
            collect(squares_of, qs.at[0], qr.at[0])
            squares = SQ[0]
            for g in range(1, F):
                squares = squares + SQ[g]
            S[z] = lax.rsqrt(squares + EPSILON)
            s_copy(z).start()
            widen(z)

        spread(squares_of, qs.at[0], qr.at[0])
        if hub:
            far, last = R - 1 - z, R - 1 - mate
            t_copy(z).start()
            send(IN, z, 0)
            send(OUT, z, 0, 1, 2)
            send(IN, z, 1)
            send(OUT, z, 3)
            relay(IN, mate, 0)
            relay(IN, mate, 1)
            relay(OUT, far, 0)
            scale()
            own = gram(z, z)
            relay(IN, mate, 2)
            s_copy(mate).wait_recv()
            s_copy(mate).start()
            widen(mate)
            relay(OUT, far, 1)
            push(own)
            t_copy(mate).wait_recv()
            t_copy(mate).start()
            relay(OUT, last, 0)
            relay(IN, mate, 3)
            relay(OUT, last, 1)
            relay(IN, mate, 4)
            send(IN, z, 2, 3, 4)
            relay(OUT, last, 2)
            send(OUT, z, 4)
            near = gram(mate, z)
            finish(own)
            push(near)
            s_copy(far).wait_recv()
            s_copy(last).wait_recv()
            widen(far)
            widen(last)
            t_copy(far).wait_recv()
            t_copy(last).wait_recv()
            one = gram(last, z, 0, 3)
            two = gram(last, mate, 0, 3)
            relay(OUT, last, 3)
            push(one, two)
            relay(OUT, last, 4)
            three = gram(last, z, 3, 2)
            four = gram(last, mate, 3, 2)
            finish(near, to=0)
            push(three, four)
            relay(OUT, far, 2)
            relay(OUT, far, 3)
            finish(two, to=1, mine=False, later=True)
            finish(one, to=2, later=True)
            five = gram(far, z, 0, 3)
            push(five)
            sums(one, to=2)
            sums(two, to=1, mine=False)
            finish(four, to=1, mine=False, later=True)
            finish(three, to=2, later=True)
            relay(OUT, far, 4)
            six = gram(far, z, 3, 2)
            push(six)
            sums(three, to=2)
            sums(four, to=1, mine=False)
            finish(five)
            finish(six)
            settle()
            g_ref[...] = lax.dot_general(
                HB[...].reshape(R * n, n), X[...].reshape(R * n, w), FIRST,
                preferred_element_type=F32,
            )
        else:
            far, last = R - 1 - mate, R - 1 - z
            send(IN, z, 0, 1, 2)
            scale()
            t_copy(z).start()
            send(IN, z, 3, 4)
            own = gram(z, z)
            push(own)
            here(mate, 0, 1, 2, 3)
            here(far, 0, 1)
            here(last, 0, 1, 2)
            finish(own)
            g_ref[...] = lax.dot_general(
                HB[z], X[z].reshape(n, w), FIRST, preferred_element_type=F32
            )
            here(mate, 4)
            here(last, 3, 4)
            receive(0, 0)
            receive(0, 1)
            here(far, 2)
            receive(2, 0)
            receive(1, 0)
            here(far, 3)
            apply(0, mate)
            receive(2, 1)
            receive(1, 1)
            totals()
            apply(1, last)
            apply(2, far)

        drained(SQ.at[pl.ds(0, F - 1)], qs.at[0], qr.at[0])
        drained(T.at[pl.ds(0, 2 if hub else 1)], ts.at[0], tr.at[0])
        drained(X.at[pl.ds(0, 2 if hub else 1)], xs.at[IN], xr.at[0, 0])
        drained(S.at[pl.ds(0, 2 if hub else 1)], ss.at[0], sr.at[0])
        sent = pl.ds(0, pieces[-1][4])
        drained(CP.at[0, sent], ps.at[0], pr.at[0])

        @pl.when(core == 0)
        def _():
            drained(CS.at[0, 0, sent], cs.at[0], cr.at[0])
            drained(CS.at[0, pl.ds(0, 2), sent], cs.at[1], cr.at[0])
            radial_out().wait_recv()

        @pl.when(core == 1)
        def _():
            drained(CS.at[0, 0, sent], cs.at[1], cr.at[0])
            radial_out().wait_send()

        rows = 2 * QUARTER * (1 if hub else F - 1)
        drained(CP.at[0, pl.ds(0, rows)], ds.at[0], dr.at[0])
        for part in range(2):
            @pl.when(core == part)
            def _():
                for q in range(1, 3):
                    share(q, part).wait_send()


        if hub:
            @pl.when(core == 1)
            def _():
                for q in range(2):
                    end_sums(q).wait_send()

            drained(X.at[pl.ds(0, 3)], xs.at[OUT], xr.at[0, 0])

    @pl.when(is_hub)
    def _():
        program(True)

    @pl.when(is_end)
    def _():
        program(False)

    factor = 4.0 * D / (n * R)
    loss_ref[...] = (D / (n * R)) * RB[1:2]
    scaling = to_column(S[z][:1])
    radial = to_column(RB[:1])
    g_ref[...] = (factor * scaling) * (g_ref[...] - (radial * scaling) * x_ref[...])


def fused(R, F, student, teacher):
    n, w = student.shape
    wt = teacher.shape[1]
    NC = n // CHUNK
    big, small = rows_of(3 * CHUNK), rows_of(n - 3 * CHUNK)
    total = 2 * rows_of(n) + 3 * (big + small)
    dma = pltpu.SemaphoreType.DMA
    vmem = pl.BlockSpec(memory_space=pltpu.VMEM)
    hbm = pl.BlockSpec(memory_space=pltpu.HBM)
    loss, grad = pl.pallas_call(
        functools.partial(kernel, R, F, NC),
        out_shape=(
            jax.ShapeDtypeStruct((1, n), F32),
            jax.ShapeDtypeStruct((n, w), F32),
        ),
        in_specs=[hbm, hbm],
        out_specs=(vmem, vmem),
        scratch_shapes=[
            pltpu.VMEM((n, w), F32),
            pltpu.VMEM((R, NC, CHUNK, w), BF16),
            pltpu.VMEM((R, n, wt), BF16),
            pltpu.VMEM((F, 8, n), F32),
            pltpu.VMEM((R, 8, n), F32),
            pltpu.VMEM((2, total, LANES), BF16),
            pltpu.VMEM((total, LANES), BF16),
            pltpu.VMEM((2, 2, total, LANES), BF16),
            pltpu.VMEM((3, 2, F * QUARTER, LANES), BF16),
            pltpu.VMEM((2, 8, n), F32),
            pltpu.VMEM((8, n), F32),
            pltpu.VMEM((R, n, n), F32),
            pltpu.VMEM((R, n, n), BF16),
            pltpu.VMEM((1, n), F32),
            dma((2,)),
            dma((2,)), dma((R, NC)),
            dma((1,)), dma((R,)),
            dma((1,)), dma((R,)),
            dma((1,)), dma((1,)),
            dma((1,)), dma((8,)), dma((2,)), dma((8,)),
            dma((1,)), dma((6,)), dma((2,)), dma((2,)), dma((6,)), dma((2,)),
            dma((1,)), dma((1,)),
        ],
        compiler_params=pltpu.CompilerParams(
            collective_id=0, has_side_effects=True, vmem_limit_bytes=48 * 2**20
        ),
    )(pltpu.with_memory_space_constraint(student, pltpu.HBM), pltpu.with_memory_space_constraint(teacher, pltpu.HBM))
    return loss.reshape(n), grad


def solution(mesh):
    R, F = mesh.shape["rows"], mesh.shape["feat"]
    body = functools.partial(fused, R, F) if R == 4 and F == 4 else ring
    in_specs = (P(("groups", "rows"), "feat"), P(("groups", "rows"), "feat"))
    out_specs = (P(("groups", "rows")), P(("groups", "rows"), "feat"))
    return jax.shard_map(
        body, mesh=mesh, in_specs=in_specs, out_specs=out_specs, check_vma=False
    )
```

```python
import functools

import jax
import jax.numpy as jnp
from jax import lax
from jax.experimental import pallas as pl
from jax.experimental.pallas import tpu as pltpu
from jax.sharding import PartitionSpec as P

D = 4096
EPSILON = 1e-06
CHUNK = 32
LANES = 128
QUARTER = 32
LAST = (((1,), (1,)), ((), ()))
FIRST = (((0,), (0,)), ((), ()))
F32 = jnp.float32
BF16 = jnp.bfloat16
MESH = pl.DeviceIdType.MESH


def shifted(block, axis, distance):
    devices = range(lax.axis_size(axis))
    route = [((i - distance) % len(devices), i) for i in devices]
    return lax.ppermute(block, axis, route)


def ring(student, teacher):
    cycle = lax.axis_size("rows")
    rows_here = student.shape[0]
    width = student.shape[1]
    embeds = rows_here * cycle
    squares = lax.psum(jnp.sum(student * student, axis=1), "feat")
    scaling = lax.rsqrt(squares + EPSILON)
    unit = student * scaling[:, None]
    unit_half = unit.astype(BF16)
    packed = jnp.concatenate([unit_half, teacher], axis=1)

    def absorb(carry, visitor):
        losses, pulled = carry
        other_unit = visitor[:, :width]
        other_teacher = visitor[:, width:]
        student_term = lax.dot_general(
            unit_half, other_unit, LAST, preferred_element_type=F32
        )
        teacher_term = lax.dot_general(
            teacher, other_teacher, LAST, preferred_element_type=F32
        )
        differ = lax.psum((student_term - teacher_term).astype(BF16), "feat").astype(F32)
        losses = losses + jnp.sum(differ * differ, axis=1)
        pulled = pulled + jnp.dot(
            differ.astype(BF16), other_unit, preferred_element_type=F32
        )
        return (losses, pulled)

    carry = (jnp.zeros((rows_here,), F32), jnp.zeros((rows_here, width), F32))
    carry = absorb(carry, packed)

    def turn(step, state):
        inner, visitor = state
        visitor = shifted(visitor, "rows", 1)
        return (absorb(inner, visitor), visitor)

    carry, visitor = lax.fori_loop(0, cycle - 1, turn, (carry, packed))
    losses, pulled = carry
    radial = lax.psum(jnp.sum(pulled * unit, axis=1), "feat")
    factor = 4.0 * D / embeds
    student_grad = factor * scaling[:, None] * (pulled - radial[:, None] * unit)
    return (D / embeds * losses, student_grad)


def rows_of(m):
    return -(-(m + m // 4) // 16) * 16


def kernel(
    R, F, NC, x_hbm, t_hbm, loss_ref, g_ref,
    x_ref, X, T, SQ, S, CP, CQ, CS, DE, RL, RB, SB, HB, rad_ref,
    ins, xs, xr, ts, tr, ss, sr, qs, qr, ps, pr, cs, cr, ds, dr, ls, lr, hr, ks, bs, br,
):
    z = lax.axis_index("rows")
    f = lax.axis_index("feat")
    core = lax.rem(f, 2)
    chip = lax.div(f, 2)
    n, w = x_ref.shape
    rc = n // NC
    RL[...] = jnp.zeros_like(RL)
    mate = z + 1 - 2 * lax.rem(z, 2)
    is_hub = jnp.logical_or(z == 1, z == 2)
    is_end = jnp.logical_not(is_hub)
    IN, OUT = 0, 1

    bar = pltpu.get_barrier_semaphore()
    for p in range(1, F):
        pl.semaphore_signal(
            bar, inc=1, device_id={"feat": lax.rem(f + p, F)}, device_id_type=MESH
        )
    pl.semaphore_signal(bar, inc=1, device_id={"rows": mate}, device_id_type=MESH)

    @pl.when(is_hub)
    def _():
        pl.semaphore_signal(bar, inc=1, device_id={"rows": R - 1 - z}, device_id_type=MESH)

    x_in = pltpu.make_async_copy(x_hbm, x_ref, ins.at[0])
    t_in = pltpu.make_async_copy(t_hbm, T.at[z], ins.at[1])
    x_in.start()
    t_in.start()

    eye = lax.broadcasted_iota(jnp.int32, (n, n), 0) == lax.broadcasted_iota(
        jnp.int32, (n, n), 1
    )

    def to_row(column):
        return jnp.sum(jnp.where(eye, column, 0.0), axis=0, keepdims=True)

    def to_column(row):
        return jnp.sum(jnp.where(eye, row, 0.0), axis=1, keepdims=True)

    x_in.wait()
    x = x_ref[...]
    X[z] = x.astype(BF16).reshape(NC, rc, w)
    SQ[f] = jnp.broadcast_to(to_row(jnp.sum(x * x, axis=1, keepdims=True)), (8, n))
    t_in.wait()
    pl.semaphore_wait(bar, F + is_hub.astype(jnp.int32))

    def pack(value):
        m = value.shape[0]
        q = m // 4
        rest = [value[i * q:(i + 1) * q, LANES:] for i in range(4)]
        return jnp.concatenate([value[:, :LANES], jnp.concatenate(rest, axis=1)], axis=0)

    def unpack(value, m):
        q = m // 4
        t = n - LANES
        rest = [value[m:m + q, i * t:(i + 1) * t] for i in range(4)]
        return jnp.concatenate([value[:m], jnp.concatenate(rest, axis=0)], axis=1)

    def remote(src, dst, send, recv, device):
        return pltpu.make_async_remote_copy(
            src_ref=src, dst_ref=dst, send_sem=send, recv_sem=recv,
            device_id=device, device_id_type=MESH,
        )

    def spread(ref_of, send, recv):
        for p in range(1, F):
            remote(
                ref_of(f), ref_of(f), send, recv, {"feat": lax.rem(f + p, F)}
            ).start()

    def collect(ref_of, send, recv):
        ref = ref_of(pl.ds(0, F - 1))
        remote(ref, ref, send, recv, feat_x).wait_recv()

    def drained(ref, send, recv):
        remote(ref, ref, send, recv, feat_x).wait_send()

    squares_of = lambda g: SQ.at[g]
    feat_x = {"feat": lax.rem(f + 2, F)}
    feat_sib = {"feat": f + 1 - 2 * core}
    feat_diag = {"feat": F - 1 - f}

    def program(hub):
        def device(d):
            if not hub or d == OUT:
                return {"rows": mate}
            return {"rows": R - 1 - z}

        def x_copy(d, src, c):
            ref = X.at[src, c]
            return remote(ref, ref, xs.at[d], xr.at[src, c], device(d))

        def t_copy(src):
            ref = T.at[src]
            return remote(ref, ref, ts.at[0], tr.at[src], device(IN))

        def s_copy(src):
            ref = S.at[src]
            return remote(ref, ref, ss.at[0], sr.at[src], device(IN))

        def send(d, src, *chunks):
            for c in chunks:
                x_copy(d, src, c).start()

        def here(src, *chunks):
            for c in chunks:
                x_copy(IN, src, c).wait_recv()

        def relay(d, src, c):
            here(src, c)
            send(d, src, c)

        pieces = []

        def spot(c, m):
            return lax.broadcasted_iota(jnp.int32, (m, n), 0) + c * rc == (
                lax.broadcasted_iota(jnp.int32, (m, n), 1)
            )

        def widen(src):
            column = jnp.sum(jnp.where(spot(0, n), S[src][:1], 0.0), axis=1, keepdims=True)
            SB[src] = jnp.broadcast_to(column, (n, n))

        def column_of(src, c, m):
            return SB[src, pl.ds(c * rc, m)]

        def halve(slot):
            at = pieces[slot][0]
            return remote(CP.at[1 - core, at], CQ.at[at], ps.at[0], pr.at[slot], feat_sib)

        def whole(slot, to, kind):
            at = pieces[slot][0]
            ref = CS.at[chip, kind, at]
            return remote(
                ref, ref, cs.at[0 if to is feat_sib else 1], cr.at[slot], to
            )

        def gram(src, by, c=0, k=NC):
            m = k * rc
            cosine = lax.dot_general(
                X[src, pl.ds(c, k)].reshape(m, w), X[by].reshape(n, w),
                LAST, preferred_element_type=F32,
            )
            cosine = cosine * S[by][:1] * column_of(src, c, m)
            term = cosine - lax.dot_general(
                T[src, pl.ds(c * rc, m)], T[by], LAST, preferred_element_type=F32
            )
            slot = len(pieces)
            start = 0 if slot == 0 else pieces[-1][4]
            stop = start + rows_of(m)
            used = pl.ds(start, m + m // 4)
            pieces.append((pl.ds(start, stop - start), c, k, src, stop, used))
            CP[0, used] = pack(term).astype(BF16)
            CP[1, used] = pack(cosine).astype(BF16)
            halve(slot).start()
            return slot

        def push(*slots):
            for slot in slots:
                used = pieces[slot][5]
                halve(slot).wait_recv()
                CS[chip, core, used] = (
                    CP[core, used].astype(F32) + CQ[used].astype(F32)
                ).astype(BF16)

                @pl.when(core == 0)
                def _():
                    for to in (feat_x, feat_diag, feat_sib):
                        whole(slot, to, 0).start()

                @pl.when(core == 1)
                def _():
                    whole(slot, feat_x, 1).start()

        def arrive(slot):
            at = pieces[slot][0]

            @pl.when(core == 0)
            def _():
                ref = CS.at[0, 0, at]
                remote(ref, ref, cs.at[0], cr.at[slot], feat_x).wait_recv()

            @pl.when(core == 1)
            def _():
                size = pieces[slot][4] - pieces[slot][0].start
                ref = CP.at[0, pl.ds(0, 3 * size)]
                remote(ref, ref, cs.at[0], cr.at[slot], feat_x).wait_recv()

        def summed(slot, kind):
            used, m = pieces[slot][5], pieces[slot][2] * rc
            return unpack(CS[0, kind, used].astype(F32) + CS[1, kind, used].astype(F32), m)

        def deliver(q, c, k, half):
            for part, (lo, hi) in enumerate(((0, 3), (3, NC))):
                if c <= lo and hi <= c + k:
                    def fill():
                        DE[q, part, used_of(part)] = pack(
                            half()[(lo - c) * rc:(hi - c) * rc]
                        ).astype(BF16)
                        (end_half if q else end_differ)(q, part).start()

                    if q:
                        pl.when(core == part)(fill)
                    else:
                        fill()

        def finish(slot, to=None, mine=True, later=False):
            _, c, k, src, _, _ = pieces[slot]
            m = k * rc
            arrive(slot)
            differ = summed(slot, 0)
            if to is not None:
                deliver(
                    to, c, k,
                    lambda: differ * (S[z][:1] if mine else column_of(src, c, m)),
                )
            if mine:
                HB[src, pl.ds(c * rc, m)] = (differ * column_of(src, c, m)).astype(BF16)
            if not later:
                sums(slot, to, mine)

        def sums(slot, to=None, mine=True):
            _, c, k, src, _, _ = pieces[slot]
            m = k * rc

            @pl.when(core == 1)
            def _():
                differ = summed(slot, 0)
                squared = differ * differ
                inner = differ * summed(slot, 1)
                loss = jnp.sum(squared, axis=0, keepdims=True)
                radial = jnp.sum(inner, axis=0, keepdims=True)
                if mine and slot == 0:
                    rad_ref[...] = radial
                    loss_ref[...] = loss
                elif mine:
                    rad_ref[...] += radial
                    loss_ref[...] += loss
                if to is not None:
                    if mine:
                        loss, radial = (
                            jnp.sum(
                                jnp.where(spot(c, m), jnp.sum(v, axis=1, keepdims=True), 0.0),
                                axis=0, keepdims=True,
                            )
                            for v in (squared, inner)
                        )
                    RL[to // 2, 0:1] += radial
                    RL[to // 2, 1:2] += loss
                    if to > 0 and c + k == NC:
                        end_sums(to // 2).start()

        def radial_out():
            return remote(RB, RB, bs.at[0], br.at[0], feat_sib)

        def settle():
            @pl.when(core == 1)
            def _():
                RB[0:1] = rad_ref[...]
                RB[1:2] = loss_ref[...]
                radial_out().start()

        def used_of(part):
            m = (3 if part == 0 else NC - 3) * rc
            return pl.ds(0, m + m // 4)

        def end_of(q):
            return {"rows": mate if q < 2 else R - 1 - mate}

        def quarter(q, part, g):
            return DE.at[q, part, pl.ds(pl.multiple_of(g * QUARTER, QUARTER), QUARTER)]

        def end_differ(q, part):
            ref = quarter(q, part, f)
            return remote(ref, ref, ds.at[0], dr.at[2 * q + part], end_of(q))

        def end_sums(q):
            return remote(RL.at[q], RL.at[q], ls.at[q], lr.at[q], end_of(2 * q))

        def half_of(q, part):
            return DE.at[q, part, pl.ds(0, rows_of((3 if part == 0 else NC - 3) * rc))]

        def end_half(q, part):
            ref = half_of(q, part)
            return remote(ref, ref, ks.at[q - 1], dr.at[2 * q + part], end_of(q))

        def share(q, part):
            ref = half_of(q, part)
            return remote(ref, ref, ks.at[q - 1], hr.at[2 * q + part], feat_sib)

        def receive(q, part):
            if q:
                @pl.when(core == part)
                def _():
                    end_half(q, part).wait_recv()
                    share(q, part).start()

                return
            end_differ(q, part).wait_recv()
            spread(lambda g: quarter(q, part, g), ds.at[0], hr.at[2 * q + part])

        def totals():
            @pl.when(core == 1)
            def _():
                for side in range(2):
                    end_sums(side).wait_recv()
                    rad_ref[...] += RL[side, 0:1]
                    loss_ref[...] += RL[side, 1:2]

            settle()

        def apply(q, src):
            for part in range(2 if q else 0):
                @pl.when(core != part)
                def _():
                    share(q, part).wait_recv()

            for part in range(0 if q else 2):
                ref = DE.at[q, part, pl.ds(0, (F - 1) * QUARTER)]
                remote(ref, ref, ds.at[0], hr.at[2 * q + part], feat_x).wait_recv()
            half = jnp.concatenate([
                unpack(DE[q, part, used_of(part)].astype(F32), (3 if part == 0 else NC - 3) * rc)
                for part in range(2)
            ]).astype(BF16)
            if q == 2:
                early = (NC - 1) * rc
                g_ref[...] += jnp.dot(
                    half[:, :early], X[src, pl.ds(0, NC - 1)].reshape(early, w),
                    preferred_element_type=F32,
                )
                here(src, NC - 1)
                g_ref[...] += jnp.dot(
                    half[:, early:], X[src, NC - 1], preferred_element_type=F32
                )
                return
            g_ref[...] += lax.dot_general(
                half, X[src].reshape(n, w),
                FIRST if q == 1 else (((1,), (0,)), ((), ())), preferred_element_type=F32,
            )

        def scale():
            collect(squares_of, qs.at[0], qr.at[0])
            squares = SQ[0]
            for g in range(1, F):
                squares = squares + SQ[g]
            S[z] = lax.rsqrt(squares + EPSILON)
            s_copy(z).start()
            widen(z)

        spread(squares_of, qs.at[0], qr.at[0])
        if hub:
            far, last = R - 1 - z, R - 1 - mate
            t_copy(z).start()
            send(IN, z, 0)
            send(OUT, z, 0, 1, 2)
            send(IN, z, 1)
            send(OUT, z, 3)
            relay(IN, mate, 0)
            relay(IN, mate, 1)
            relay(OUT, far, 0)
            scale()
            own = gram(z, z)
            relay(IN, mate, 2)
            s_copy(mate).wait_recv()
            s_copy(mate).start()
            widen(mate)
            relay(OUT, far, 1)
            push(own)
            t_copy(mate).wait_recv()
            t_copy(mate).start()
            relay(OUT, last, 0)
            relay(IN, mate, 3)
            relay(OUT, last, 1)
            relay(IN, mate, 4)
            send(IN, z, 2, 3, 4)
            relay(OUT, last, 2)
            send(OUT, z, 4)
            near = gram(mate, z)
            finish(own)
            push(near)
            s_copy(far).wait_recv()
            s_copy(last).wait_recv()
            widen(far)
            widen(last)
            t_copy(far).wait_recv()
            t_copy(last).wait_recv()
            one = gram(last, z, 0, 3)
            two = gram(last, mate, 0, 3)
            relay(OUT, last, 3)
            push(one, two)
            relay(OUT, last, 4)
            three = gram(last, z, 3, 2)
            four = gram(last, mate, 3, 2)
            finish(near, to=0)
            push(three, four)
            relay(OUT, far, 2)
            relay(OUT, far, 3)
            finish(two, to=1, mine=False, later=True)
            finish(one, to=2, later=True)
            five = gram(far, z, 0, 3)
            push(five)
            sums(one, to=2)
            sums(two, to=1, mine=False)
            finish(four, to=1, mine=False, later=True)
            finish(three, to=2, later=True)
            relay(OUT, far, 4)
            six = gram(far, z, 3, 2)
            push(six)
            sums(three, to=2)
            sums(four, to=1, mine=False)
            finish(five)
            finish(six)
            settle()
            g_ref[...] = lax.dot_general(
                HB[...].reshape(R * n, n), X[...].reshape(R * n, w), FIRST,
                preferred_element_type=F32,
            )
        else:
            far, last = R - 1 - mate, R - 1 - z
            send(IN, z, 0, 1, 2)
            scale()
            t_copy(z).start()
            send(IN, z, 3, 4)
            own = gram(z, z)
            push(own)
            here(mate, 0, 1, 2, 3)
            here(far, 0, 1)
            here(last, 0, 1, 2)
            finish(own)
            g_ref[...] = lax.dot_general(
                HB[z], X[z].reshape(n, w), FIRST, preferred_element_type=F32
            )
            here(mate, 4)
            here(last, 3, 4)
            receive(0, 0)
            receive(0, 1)
            here(far, 2)
            receive(2, 0)
            receive(1, 0)
            here(far, 3)
            apply(0, mate)
            receive(2, 1)
            receive(1, 1)
            totals()
            apply(1, last)
            apply(2, far)

        drained(SQ.at[pl.ds(0, F - 1)], qs.at[0], qr.at[0])
        drained(T.at[pl.ds(0, 2 if hub else 1)], ts.at[0], tr.at[0])
        drained(X.at[pl.ds(0, 2 if hub else 1)], xs.at[IN], xr.at[0, 0])
        drained(S.at[pl.ds(0, 2 if hub else 1)], ss.at[0], sr.at[0])
        sent = pl.ds(0, pieces[-1][4])
        drained(CP.at[0, sent], ps.at[0], pr.at[0])

        @pl.when(core == 0)
        def _():
            drained(CS.at[0, 0, sent], cs.at[0], cr.at[0])
            drained(CS.at[0, pl.ds(0, 2), sent], cs.at[1], cr.at[0])
            radial_out().wait_recv()

        @pl.when(core == 1)
        def _():
            drained(CS.at[0, 0, sent], cs.at[1], cr.at[0])
            radial_out().wait_send()

        rows = 2 * QUARTER * (1 if hub else F - 1)
        drained(CP.at[0, pl.ds(0, rows)], ds.at[0], dr.at[0])
        for part in range(2):
            @pl.when(core == part)
            def _():
                for q in range(1, 3):
                    share(q, part).wait_send()


        if hub:
            @pl.when(core == 1)
            def _():
                for q in range(2):
                    end_sums(q).wait_send()

            drained(X.at[pl.ds(0, 3)], xs.at[OUT], xr.at[0, 0])

    @pl.when(is_hub)
    def _():
        program(True)

    @pl.when(is_end)
    def _():
        program(False)

    factor = 4.0 * D / (n * R)
    loss_ref[...] = (D / (n * R)) * RB[1:2]
    scaling = SB[z][:, :1]
    radial = to_column(RB[:1])
    g_ref[...] = (factor * scaling) * (g_ref[...] - (radial * scaling) * x_ref[...])


def fused(R, F, student, teacher):
    n, w = student.shape
    wt = teacher.shape[1]
    NC = n // CHUNK
    big, small = rows_of(3 * CHUNK), rows_of(n - 3 * CHUNK)
    total = 2 * rows_of(n) + 3 * (big + small)
    dma = pltpu.SemaphoreType.DMA
    vmem = pl.BlockSpec(memory_space=pltpu.VMEM)
    hbm = pl.BlockSpec(memory_space=pltpu.HBM)
    loss, grad = pl.pallas_call(
        functools.partial(kernel, R, F, NC),
        out_shape=(
            jax.ShapeDtypeStruct((1, n), F32),
            jax.ShapeDtypeStruct((n, w), F32),
        ),
        in_specs=[hbm, hbm],
        out_specs=(vmem, vmem),
        scratch_shapes=[
            pltpu.VMEM((n, w), F32),
            pltpu.VMEM((R, NC, CHUNK, w), BF16),
            pltpu.VMEM((R, n, wt), BF16),
            pltpu.VMEM((F, 8, n), F32),
            pltpu.VMEM((R, 8, n), F32),
            pltpu.VMEM((2, total, LANES), BF16),
            pltpu.VMEM((total, LANES), BF16),
            pltpu.VMEM((2, 2, total, LANES), BF16),
            pltpu.VMEM((3, 2, F * QUARTER, LANES), BF16),
            pltpu.VMEM((2, 8, n), F32),
            pltpu.VMEM((8, n), F32),
            pltpu.VMEM((R, n, n), F32),
            pltpu.VMEM((R, n, n), BF16),
            pltpu.VMEM((1, n), F32),
            dma((2,)),
            dma((2,)), dma((R, NC)),
            dma((1,)), dma((R,)),
            dma((1,)), dma((R,)),
            dma((1,)), dma((1,)),
            dma((1,)), dma((8,)), dma((2,)), dma((8,)),
            dma((1,)), dma((6,)), dma((2,)), dma((2,)), dma((6,)), dma((2,)),
            dma((1,)), dma((1,)),
        ],
        compiler_params=pltpu.CompilerParams(
            collective_id=0, has_side_effects=True, vmem_limit_bytes=48 * 2**20
        ),
    )(pltpu.with_memory_space_constraint(student, pltpu.HBM), pltpu.with_memory_space_constraint(teacher, pltpu.HBM))
    return loss.reshape(n), grad


def solution(mesh):
    R, F = mesh.shape["rows"], mesh.shape["feat"]
    body = functools.partial(fused, R, F) if R == 4 and F == 4 else ring
    in_specs = (P(("groups", "rows"), "feat"), P(("groups", "rows"), "feat"))
    out_specs = (P(("groups", "rows")), P(("groups", "rows"), "feat"))
    return jax.shard_map(
        body, mesh=mesh, in_specs=in_specs, out_specs=out_specs, check_vma=False
    )
```
